32 devices in a mesh: tm: 4 (over x, core), space: 8 (over z, y).
Axes of the slice: x: 2, y: 2, z: 4, core: 2. Of those that a mesh axis runs over, the one named last changes fastest.
Arguments:
- cotangent: bfloat16 [16, 64, 8192], P('tm', 'space'), may hold values from -6 to 6
- saved_mix: bfloat16 [16, 64, 8192], P('tm', 'space'), may hold values from -6 to 6
- saved_pre: bfloat16 [16, 64, 8192], P('tm', 'space'), may hold values from -8 to 8
- kernel_one: bfloat16 [4, 3, 3, 64, 64], replicated, may hold values from -0.25 to 0.25
- kernel_two: bfloat16 [4, 3, 3, 64, 64], replicated, may hold values from -0.25 to 0.25
- ref_pairs: int32 [16, 2], replicated, may hold values from 0 to 15, as said below
- frame_level: int32 [16], replicated, may hold values from 0 to 4, as said below
Outputs:
- input_grad: float32 [16, 64, 8192], P('tm', 'space')
- weight_grad_one: float32 [4, 3, 3, 64, 64], replicated
- weight_grad_two: float32 [4, 3, 3, 64, 64], replicated
The draws below stay inside these ranges and needn't reach their ends.
Inputs may be any that keep to these rules, and one draw needn't show every extreme that they name: Frame c was predicted from frames ref_pairs[c, 0] and ref_pairs[c, 1]; for a frame of level k >= 1 both have a level below k (at level 1 both name the level-0 frame); the level-0 frame names itself twice. `frame_level`: one frame has level 0 and 2**(k-1) frames have level k for k from 1 to 4; frames are stored in an order drawn from the seed.
All inputs are finite; a program needn't handle non-finite values.
Results may differ from the reference program's by a relative error of at most 0.006.
Values may be sent and summed in bfloat16 or wider, within the bound.
A program may use at most 64 MiB of HBM per device.

```python
import math
import jax
import jax.numpy as jnp
import numpy as np
from jax import lax

F = 16
LEVELS = 4
C = 64
W = 128
ROWS = 64


def gop_tables(key):
    storage = jax.random.permutation(jax.random.fold_in(key, 11), F).astype(jnp.int32)
    disp_level = np.zeros((F,), np.int32)
    disp_refs = np.zeros((F, 2), np.int32)
    for position in range(1, F):
        stride = position & -position
        disp_level[position] = LEVELS - (stride.bit_length() - 1)
        disp_refs[position, 0] = position - stride
        disp_refs[position, 1] = (position + stride) % F
    level_store = jnp.zeros((F,), jnp.int32).at[storage].set(jnp.asarray(disp_level))
    refs_store = jnp.zeros((F, 2), jnp.int32).at[storage].set(storage[jnp.asarray(disp_refs)])
    return (level_store, refs_store)


def draw_ref_pairs(key, part):
    return gop_tables(key)[1]


def draw_frame_level(key, part):
    return gop_tables(key)[0]


def block_levels(stream_key, shape, cuts, smallest, largest):
    def one(dim, blocks):
        heights = jax.random.uniform(jax.random.fold_in(jax.random.fold_in(stream_key, 6), dim), (blocks,), jnp.float32, smallest / len(cuts), largest / len(cuts))
        return jnp.repeat(jnp.exp(heights), shape[dim] // blocks).reshape((-1,) + (1,) * (len(shape) - dim - 1))

    loudness = one(*cuts[0])
    for cut in cuts[1:]:
        loudness = loudness * one(*cut)
    return loudness


def scatter_about(stream_key, shape, spread, limit, shards=(), kind=jnp.bfloat16):
    factor_of = block_levels(stream_key, shape, shards, -0.22, 0.18) if shards else 1.0
    entries = jax.random.normal(stream_key, shape, jnp.float32) * spread * factor_of
    return jnp.minimum(jnp.maximum(entries, -limit), limit).astype(kind)


def setup_inputs(seed: int = 0) -> dict:
    keys = jax.random.split(jax.random.key(seed), 8)
    return {
        "cotangent": scatter_about(keys[0], (F, ROWS, W * C), 1.0, 6.0, ((0, 4), (1, 8))),
        "saved_mix": scatter_about(keys[1], (F, ROWS, W * C), 1.0, 6.0, ((0, 4), (1, 8))),
        "saved_pre": scatter_about(keys[2], (F, ROWS, W * C), 1.5, 8.0, ((0, 4), (1, 8))),
        "kernel_one": scatter_about(keys[3], (LEVELS, 3, 3, C, C), (9 * C) ** -0.5, 0.25),
        "kernel_two": scatter_about(keys[4], (LEVELS, 3, 3, C, C), (9 * C) ** -0.5, 0.25),
        "ref_pairs": draw_ref_pairs(jax.random.fold_in(keys[7], 71), 0),
        "frame_level": draw_frame_level(jax.random.fold_in(keys[7], 71), 0),
    }


def shifted(field, row_tap, col_tap):
    padded = jnp.pad(field, ((0, 0), (1, 1), (1, 1), (0, 0)))
    return padded[:, row_tap:row_tap + ROWS, col_tap:col_tap + W]

def conv_full(field, kernel):
    running = jnp.zeros(field.shape[:3] + (C,), jnp.float32)
    for row_tap in range(3):
        for col_tap in range(3):
            moved = shifted(field, row_tap, col_tap).reshape(-1, C)
            running = running + jnp.dot(moved, kernel[row_tap, col_tap], preferred_element_type=jnp.float32).reshape(running.shape)
    return running

def adjoint(field, kernel):
    return conv_full(field, jnp.transpose(kernel[::-1, ::-1], (0, 1, 3, 2)))

def correlate_full(field, cot):
    cot_wide = cot.astype(jnp.float32)
    rows_out = []
    for row_tap in range(3):
        taps = []
        for col_tap in range(3):
            moved = shifted(field, row_tap, col_tap).astype(jnp.float32)
            taps.append(jnp.einsum('frwi,frwo->fio', moved, cot_wide, precision=lax.Precision.HIGHEST))
        rows_out.append(jnp.stack(taps, axis=1))
    return jnp.stack(rows_out, axis=1)

def reference(cotangent, saved_mix, saved_pre, kernel_one, kernel_two, ref_pairs, frame_level):
    shape_four = (F, ROWS, W, C)
    preact = saved_pre.astype(jnp.float32).reshape(shape_four)
    sigmoid_pre = jax.nn.sigmoid(preact)
    act_slope = sigmoid_pre * (1.0 + preact * (1.0 - sigmoid_pre))
    act_out = (preact * sigmoid_pre).astype(jnp.bfloat16)
    cot_total = cotangent.astype(jnp.float32).reshape(shape_four)
    kept_grad = jnp.zeros(shape_four, jnp.bfloat16)
    frame_ids = jnp.arange(F, dtype=jnp.int32)
    for level_now in range(LEVELS, 0, -1):
        chosen = jnp.nonzero(frame_level == level_now, size=2 ** (level_now - 1))[0].astype(jnp.int32)
        cot_round = cot_total[chosen].astype(jnp.bfloat16)
        slot_grad = (adjoint(cot_round, kernel_two[level_now - 1]) * act_slope[chosen]).astype(jnp.bfloat16)
        to_refs = adjoint(slot_grad, kernel_one[level_now - 1]).astype(jnp.bfloat16)
        kept_grad = kept_grad.at[chosen].set(slot_grad)
        first_ref = ref_pairs[chosen, 0]
        second_ref = ref_pairs[chosen, 1]
        weights = 0.5 * ((first_ref[:, None] == frame_ids[None, :]).astype(jnp.float32) + (second_ref[:, None] == frame_ids[None, :]).astype(jnp.float32))
        added = jnp.dot(weights.T.astype(jnp.bfloat16), to_refs.reshape(to_refs.shape[0], -1), preferred_element_type=jnp.float32)
        cot_total = cot_total + added.reshape(shape_four)
    final_cot = cot_total.astype(jnp.bfloat16)
    level_hot = (frame_level[:, None] == jnp.arange(1, LEVELS + 1, dtype=jnp.int32)[None, :]).astype(jnp.float32)
    scale = 1.0 / math.sqrt(ROWS * W)
    mix_four = saved_mix.reshape(shape_four)
    per_one = correlate_full(mix_four, kept_grad)
    per_two = correlate_full(act_out, final_cot)
    grad_one = scale * lax.optimization_barrier(jnp.sum(level_hot[:, :, None, None, None, None] * per_one[:, None], axis=0))
    grad_two = scale * lax.optimization_barrier(jnp.sum(level_hot[:, :, None, None, None, None] * per_two[:, None], axis=0))
    return (cot_total.reshape(F, ROWS, W * C), grad_one, grad_two)
```

```python
import functools
import math

import jax
import jax.numpy as jnp
from jax import lax
from jax.experimental import pallas as pl
from jax.experimental.pallas import tpu as pltpu
from jax.sharding import PartitionSpec as P

BF = jnp.bfloat16
F32 = jnp.float32
I32 = jnp.int32


def div(value, n):
    return lax.shift_right_logical(value, jnp.full_like(value, n.bit_length() - 1))


def mod(value, n):
    return jnp.bitwise_and(value, n - 1)


def iota(shape, dim):
    return lax.broadcasted_iota(I32, shape, dim)


def nt_dot(a, b):
    return lax.dot_general(a, b, (((1,), (1,)), ((), ())), preferred_element_type=F32)


def nn_dot(a, b):
    return jnp.dot(a, b, preferred_element_type=F32)


def segments(levels):
    segs = []
    low = 0
    for level in range(levels - 1, 1, -1):
        count = 2 ** (level - 1)
        segs.append((low, count))
        low += count
    segs.append((low, 2))
    return segs


def group_kernel(nx, ns, levels, cot_ref, pre_ref, mix_ref, lev_ref, pairs_ref, k1_ref, k2_ref,
                 grad_ref, wg_ref, rawx, raws, pre_s, pre_r, mix_s, mix_r, hal_s, hal_r, cot, pre,
                 mix, act, slope, work, refs, im, imc, conv_out, out_s, out_r, rhs_buf, bands, kpad,
                 perm, comb, sel, back, part, ab_s, ab_r, c_s, c_r, e_b, ssem, rsem):
    tm = lax.axis_index("tm")
    sp = lax.axis_index("space")
    xi = tm // 2
    core = tm % 2
    nt = 2 * nx
    fl, rows, width = cot_ref.shape
    frames = fl * nt
    half = frames // 2
    lanes = cot.shape[2]
    own = lanes - 1536
    span = own + 1024
    mid = slice(256, 256 + span)
    quads = lanes // 256
    inner_q = quads - 2
    wide = own // 256
    shard = part.shape[2]
    down = (sp + 1) % ns
    up = (sp + ns - 1) % ns
    sib = (xi * 2 + 1 - core, sp)
    chip = rawx.shape[4] - 1024
    tms = [((tm + d) % nt, sp) for d in range(1, nt)]
    sps = [(tm, (sp + d) % ns) for d in range(1, ns)]

    barrier = pltpu.get_barrier_semaphore()
    for peer in tms + sps:
        pl.semaphore_signal(barrier, inc=1, device_id=peer, device_id_type=pl.DeviceIdType.MESH)
    slots = [0]

    def send(src, dst, peer):
        copy = pltpu.make_async_remote_copy(
            src_ref=src, dst_ref=dst, send_sem=ssem.at[slots[0]], recv_sem=rsem.at[slots[0]],
            device_id=peer, device_id_type=pl.DeviceIdType.MESH)
        copy.start()
        slots[0] += 1
        return copy

    sources = (cot_ref, pre_ref, mix_ref)
    targets = (cot, pre, mix)

    def chip_start(x):
        start = 2 * own * x - 512 * ((x + nx - 1) // nx)
        if nx > 2:
            start = start - 512 * (x // (nx - 1))
        return start

    def window(x, c):
        return pl.ds(pl.multiple_of((2 * x + c) * own - chip_start(x), 128), span)

    def send_chips(n):
        copies = []
        for d in range(1, nx):
            x = (xi + d) % nx
            cut = pl.ds(pl.multiple_of(chip_start(x), 128), chip)
            copies.append(send(sources[n].at[:, :, cut], rawx.at[n, xi, :, :, 512 : 512 + chip],
                               (x * 2 + core, sp)))
        return copies

    def keep_own(n):
        cut = pl.ds(pl.multiple_of(chip_start(xi), 128), chip)
        rawx[n, xi, :, :, 512 : 512 + chip] = sources[n][:, :, cut]

    def pass_on(n, x):
        return send(rawx.at[n, x, :, :, window(xi, 1 - core)], raws.at[n, x], sib)

    pl.semaphore_wait(barrier, len(tms) + len(sps))
    across = [send_chips(0), send_chips(1)]
    rawx[:, :, :, :, 0:512] = jnp.zeros((3, nx, fl, rows, 512), BF)
    rawx[:, :, :, :, 512 + chip :] = jnp.zeros((3, nx, fl, rows, 512), BF)
    passed = [[], [], []]
    for n in range(2):
        keep_own(n)
        passed[n].append(pass_on(n, xi))
    for held in (cot, pre, mix, act):
        held[:, :, 0:256] = jnp.zeros((rows + 4, frames, 256), F32)
        held[:, :, lanes - 256 :] = jnp.zeros((rows + 4, frames, 256), F32)
    work[...] = jnp.zeros_like(work)

    order_row = (levels - lev_ref[...]) * frames + iota((1, frames), 1)
    order_row = order_row.astype(F32)
    eye = iota((frames, frames), 0) == iota((frames, frames), 1)
    order_col = jnp.sum(jnp.where(eye, jnp.broadcast_to(order_row, (frames, frames)), 0.0),
                        axis=1, keepdims=True)
    rank_row = jnp.sum((order_col < order_row).astype(F32), axis=0, keepdims=True)
    hot = (iota((frames, frames), 0).astype(F32) == rank_row).astype(F32)
    total = frames * rows
    m_id = iota((total, frames), 0)
    to_slot = (mod(m_id, frames) == iota((total, frames), 1)).astype(F32)
    n_id = iota((frames, total), 1)
    side = div(n_id, rows * fl * nx)
    from_core = core + side - 2 * core * side
    from_frame = ((mod(div(n_id, rows * fl), nx) * 2 + from_core) * fl + mod(div(n_id, rows), fl))
    from_hot = (from_frame == iota((frames, total), 0)).astype(F32)
    same_row = div(iota((total, total), 0), frames) == mod(iota((total, total), 1), rows)
    perm[...] = jnp.where(same_row, nn_dot(to_slot, nn_dot(hot, from_hot)), 0.0).astype(BF)
    pairs = pairs_ref[...]
    ref_hot = 0.5 * ((pairs[:, 0:1] == iota((frames, frames), 1)).astype(F32)
                     + (pairs[:, 1:2] == iota((frames, frames), 1)).astype(F32))
    mixw = nt_dot(nt_dot(hot, ref_hot), hot)
    few = rows // 2 * half
    to_low = (mod(iota((few, frames), 0), half) + half == iota((few, frames), 1)).astype(F32)
    same_few = div(iota((few, few), 0), half) == div(iota((few, few), 1), half)
    for k in range(levels):
        g = 0 if k == levels - 1 else half
        lowest = frames - 2 ** (k + 1)
        s_id = mod(iota((frames, few), 1), half) + g
        on = jnp.logical_and(s_id >= lowest, s_id < lowest + 2**k)
        pick = jnp.logical_and(s_id == iota((frames, few), 0), on).astype(F32)
        comb[k] = jnp.where(same_few, nn_dot(nn_dot(to_low, mixw), pick), 0.0).astype(BF)
    low_rows = rows * half
    local = (div(iota((fl * rows, frames), 0), rows) + tm * fl
             == iota((fl * rows, frames), 1)).astype(F32)
    local_hot = nt_dot(local, hot)
    top = jnp.sum(jnp.where(iota((fl * rows, frames), 1) < half, local_hot, 0.0),
                  axis=1, keepdims=True)
    segs = segments(levels)
    o_id = iota((frames, low_rows), 1)
    o_row = mod(iota((fl * rows, low_rows), 0), rows)
    p_id = iota((fl * rows, low_rows), 1)
    slot_of = jnp.zeros_like(o_id)
    row_of = jnp.zeros_like(p_id)
    for low, count in segs:
        here = o_id >= low * rows
        slot_of = jnp.where(here, half + low + mod(o_id - low * rows, count), slot_of)
        there = p_id >= low * rows
        row_of = jnp.where(there, div(p_id - low * rows, count), row_of)
    back[...] = jnp.where(o_row == row_of, nn_dot(
        local_hot, (slot_of == iota((frames, low_rows), 0)).astype(F32)), 0.0).astype(BF)
    for low, count in segs:
        size = rows * count
        a_id = iota((size, low_rows), 0)
        b_id = iota((size, low_rows), 1)
        sel[low * rows : low * rows + size] = jnp.logical_and(
            div(a_id, count) == div(b_id, half),
            low + mod(a_id, count) == mod(b_id, half)).astype(F32).astype(BF)

    bands[...] = jnp.zeros_like(bands)
    kpad[0:64] = jnp.zeros((64, 64), BF)
    kpad[256:320] = jnp.zeros((64, 64), BF)
    unit = (iota((64, 64), 0) == iota((64, 64), 1)).astype(F32).astype(BF)
    for n in range(2):
        for k in range(levels):
            for a in range(3):
                kpad[64:256] = (k2_ref, k1_ref)[n][k, 2 - a]
                even = nt_dot(unit, kpad[64:320]).astype(BF)
                odd = nt_dot(unit, kpad[0:256]).astype(BF)
                bands[n, k, a, 64:128, 0:128] = even[:, 128:256]
                bands[n, k, a, 128:192, 0:128] = odd[:, 128:256]
                bands[n, k, a, 192:256] = even
                bands[n, k, a, 256:320] = odd
                bands[n, k, a, 320:384, 128:256] = even[:, 0:128]
                bands[n, k, a, 384:448, 128:256] = odd[:, 0:128]

    def gather(n):
        for i, copy in enumerate(across[n]):
            copy.wait()
            passed[n].append(pass_on(n, (xi + nx - 1 - i) % nx))
        for copy in passed[n]:
            copy.wait()
        mine = (2 * xi + core) * own - chip_start(xi)
        for j in range(inner_q):
            cut = pl.ds(pl.multiple_of(mine + 256 * j, 128), 256)
            one = rawx[n, :, :, :, cut].astype(F32).reshape(total // 2, 256)
            two = raws[n, :, :, :, 256 * j : 256 * j + 256].astype(F32).reshape(total // 2, 256)
            block = jnp.concatenate((one, two), axis=0).astype(BF)
            moved = nn_dot(perm[...], block)
            targets[n][2 : 2 + rows, :, 256 * j + 256 : 256 * j + 512] = moved.reshape(
                rows, frames, 256)

    def push(k):
        g = 0 if k == levels - 1 else half
        hal_s[k, 0] = cot[2:4, g : g + half, mid].reshape(2 * half, span).astype(BF)
        hal_s[k, 1] = cot[rows : rows + 2, g : g + half, mid].reshape(2 * half, span).astype(BF)
        return [send(hal_s.at[k, 0], hal_r.at[k, 1], (tm, up)),
                send(hal_s.at[k, 1], hal_r.at[k, 0], (tm, down))]

    has_up = (sp > 0).astype(F32)
    has_down = (sp < ns - 1).astype(F32)
    column = iota((8, lanes), 1) + tm * own - 768
    inside = jnp.logical_and(column >= 0, column < own * nt).astype(F32)

    gather(0)
    flight = push(levels - 1)
    gather(1)
    across.append(send_chips(2))
    keep_own(2)
    passed[2].append(pass_on(2, xi))
    pre_s[0] = pre[2, :, mid].astype(BF)
    pre_s[1] = pre[rows + 1, :, mid].astype(BF)
    edges = [send(pre_s.at[0], pre_r.at[1], (tm, up)), send(pre_s.at[1], pre_r.at[0], (tm, down))]

    def activate(r):
        gate = has_up if r == 0 else (has_down if r == rows + 1 else 1.0)
        for g in range(0, frames, 8):
            v = pre[r + 1, g : g + 8, mid]
            sig = jax.nn.sigmoid(v)
            slope[r, g : g + 8, mid] = sig * (1.0 + v * (1.0 - sig)) * inside[:, mid] * gate
            act[r + 1, g : g + 8, mid] = v * sig

    for r in range(1, rows + 1):
        activate(r)
    for copy in edges:
        copy.wait()
    pre[1, :, mid] = pre_r[0].astype(F32) * has_up
    pre[rows + 2, :, mid] = pre_r[1].astype(F32) * has_down
    activate(0)
    activate(rows + 1)

    def fill(dest, source, g, first, count, base, width):
        for r in range(count):
            for j in range(0, width, 2):
                lo = 256 * (base + j) - 128
                one = source[first + r, g : g + 8, lo : lo + 512]
                two = source[first + r, g : g + 8, lo + 256 : lo + 768]
                dest[r, 8 * j : 8 * j + 16] = jnp.concatenate((one, two), axis=0).astype(BF)

    def conv(n, k, first, count, base, width, store):
        size = count * 8 * width
        total = None
        for a in range(3):
            lhs = im[first + a : first + a + count, 0 : 8 * width].reshape(size, 512)
            term = nn_dot(lhs, bands[n, k, a])
            total = term if total is None else total + term
        conv_out[0:size] = total
        for r in range(count):
            for j in range(width):
                at = (r * width + j) * 8
                store(first + r, base + j, conv_out[at : at + 8])

    slot_no = iota((8, 256), 0) + 8

    def correlate(k):
        g = 0 if k == levels - 1 else half
        lowest = frames - 2 ** (k + 1)
        active = jnp.logical_and(slot_no >= lowest, slot_no < lowest + 2**k)
        tall = 8 * wide
        for n in range(2):
            for r in range(rows):
                for j in range(0, wide, 2):
                    cut = 768 + 256 * j
                    if n == 0:
                        left = work[1 + r, :, cut : cut + 256]
                        right = work[1 + r, :, cut + 256 : cut + 512]
                    else:
                        left = cot[2 + r, g : g + 8, cut : cut + 256]
                        right = cot[2 + r, g : g + 8, cut + 256 : cut + 512]
                    if g:
                        left = jnp.where(active, left, 0.0)
                        right = jnp.where(active, right, 0.0)
                    rhs_buf[n, r, 8 * j : 8 * j + 16] = jnp.concatenate(
                        (left, right), axis=0).astype(BF)
        step = math.gcd(192, shard)
        for a in range(3):
            both = []
            for n in range(2):
                rhs = rhs_buf[n].reshape(rows * tall, 256)
                lhs = imc[n, 1 if g else 0, a : a + rows].reshape(rows * tall, 512)
                block = lax.dot_general(
                    lhs, rhs, (((0,), (0,)), ((), ())), preferred_element_type=F32)
                taps = block[64:256, 0:64]
                for p in range(1, 4):
                    taps = taps + block[64 * (p + 1) : 64 * (p + 4), 64 * p : 64 * p + 64]
                both.append(taps)
            joint = jnp.concatenate(both, axis=1) * (1.0 / math.sqrt(rows * ns * (own * nt // 64)))
            for i in range(0, 192, step):
                at = 192 * a + i
                value = joint[i : i + step]
                part[k, at // shard, at % shard : at % shard + step] = value
        for t in range(nt):
            ab_s[k, t] = part[k, t].astype(BF)
        return [send(ab_s.at[k, peer[0]], ab_r.at[k, tm], peer) for peer in tms]

    def second(k, copies):
        for copy in copies:
            copy.wait()
        value = part[k, tm]
        for d in range(1, nt):
            value = value + ab_r[k, (tm + d) % nt].astype(F32)
        c_s[k] = value.astype(BF)
        c_r[k, sp] = value.astype(BF)
        return [send(c_s.at[k], c_r.at[k, sp], peer) for peer in sps]

    def third(k, copies):
        for copy in copies:
            copy.wait()
        value = c_r[k, 0].astype(F32)
        for s in range(1, ns):
            value = value + c_r[k, s].astype(F32)
        e_b[k, tm] = value.astype(BF)
        return [send(e_b.at[k, tm], e_b.at[k, tm], peer) for peer in tms]

    def hand_out(low, count):
        a, b = low * rows, (low + count) * rows
        for j in range(wide):
            cut = slice(768 + 256 * j, 1024 + 256 * j)
            flat = cot[2 : 2 + rows, half:, cut].reshape(low_rows, 256).astype(BF)
            value = nn_dot(sel[a:b], flat).astype(BF)
            out_s[a:b, 256 * j : 256 * j + 256] = value
            out_r[tm, a:b, 256 * j : 256 * j + 256] = value
        return [send(out_s.at[a:b], out_r.at[tm, a:b], peer) for peer in tms]

    outs = []
    stage = {}
    for k in range(levels - 1, -1, -1):
        g = 0 if k == levels - 1 else half
        for copy in flight:
            copy.wait()
        cot[0:2, g : g + half, mid] = hal_r[k, 0].astype(F32).reshape(2, half, span) * has_up
        cot[rows + 2 : rows + 4, g : g + half, mid] = (
            hal_r[k, 1].astype(F32).reshape(2, half, span) * has_down)

        def put_grad(r, j, block):
            cut = slice(256 * j, 256 * j + 256)
            work[r, :, cut] = (block * slope[r, g : g + 8, cut]).astype(BF).astype(F32)

        def put_refs(r, j, block):
            cut = slice(256 * j, 256 * j + 256)
            refs[r, :, cut] = block * inside[:, cut]

        def combine(pieces, base, width):
            for j in range(base, base + width):
                cut = slice(256 * j, 256 * j + 256)
                block = jnp.concatenate([refs[a:b, :, cut].reshape((b - a) * 8, 256)
                                         for a, b in pieces], axis=0).astype(BF)
                extra = nn_dot(comb[k], block)
                at = 0
                for a, b in pieces:
                    size = (b - a) * half
                    cot[2 + a : 2 + b, half:, cut] += extra[at : at + size].reshape(
                        b - a, half, 256)
                    at += size

        skip = (0, 0, 1, 1)[levels - 1 - k] if levels == 4 else 0
        base, width = 1 + skip, inner_q - 2 * skip
        fill(im, cot, g, 0, rows + 4, base, width)
        conv(0, k, 0, rows // 2 + 1, base, width, put_grad)
        conv(0, k, rows // 2 + 1, rows // 2 + 1, base, width, put_grad)
        if k == 0:
            stage[k] = correlate(k)
        skip = (0, 1, 1, 2)[levels - 1 - k] if levels == 4 else 0
        base, width = 1 + skip, inner_q - 2 * skip
        fill(im, work, 0, 0, rows + 2, base, width)
        quarter = rows // 4
        conv(1, k, 0, quarter, base, width, put_refs)
        conv(1, k, rows - quarter, quarter, base, width, put_refs)
        combine([(0, quarter), (rows - quarter, rows)], base, width)
        if k > 0:
            flight = push(k - 1)
        conv(1, k, quarter, rows - 2 * quarter, base, width, put_refs)
        combine([(quarter, rows - quarter)], base, width)
        if k == levels - 1:
            fill(imc.at[1, 0], act, 0, 1, rows + 2, 3, wide)
            fill(imc.at[1, 1], act, half, 1, rows + 2, 3, wide)
            gather(2)
            trim = slice(640, 896 + own)
            mix_s[0] = mix[2, :, trim].astype(BF)
            mix_s[1] = mix[rows + 1, :, trim].astype(BF)
            edges = [send(mix_s.at[0], mix_r.at[1], (tm, up)),
                     send(mix_s.at[1], mix_r.at[0], (tm, down))]
            for copy in edges:
                copy.wait()
            mix[1, :, trim] = mix_r[0].astype(F32) * has_up
            mix[rows + 2, :, trim] = mix_r[1].astype(F32) * has_down
            fill(imc.at[0, 0], mix, 0, 1, rows + 2, 3, wide)
            fill(imc.at[0, 1], mix, half, 1, rows + 2, 3, wide)
        at = levels - 1 - k
        if at < len(segs) - 1:
            outs.append(hand_out(*segs[at]))
        if k == 0:
            outs.append(hand_out(*segs[-1]))
        if k > 0:
            stage[k] = correlate(k)
        if k + 2 < levels:
            stage[k + 2] = third(k + 2, stage[k + 2])
        if k + 1 < levels:
            stage[k + 1] = second(k + 1, stage[k + 1])
    stage[0] = second(0, stage[0])
    if levels > 1:
        stage[1] = third(1, stage[1])
    for group in outs:
        for copy in group:
            copy.wait()
    for t in range(nt):
        for j in range(wide):
            cut = slice(own * t + 256 * j, own * t + 256 * j + 256)
            plain = cot_ref[:, :, cut].astype(F32).reshape(fl * rows, 256)
            value = nn_dot(back[...], out_r[t, :, 256 * j : 256 * j + 256]) + top * plain
            grad_ref[:, cut] = value.astype(BF)
    stage[0] = third(0, stage[0])
    for k in range(levels):
        for copy in stage[k]:
            copy.wait()
        for t in range(nt):
            wg_ref[k, t] = e_b[k, t]


def on_device(cotangent, saved_mix, saved_pre, kernel_one, kernel_two, ref_pairs, frame_level):
    fl, rows, width = cotangent.shape
    nt = lax.axis_size("tm")
    nx = nt // 2
    ns = lax.axis_size("space")
    levels = kernel_one.shape[0]
    frames = fl * nt
    half = frames // 2
    own = width // nt
    lanes = own + 1536
    span = own + 1024
    quads = lanes // 256
    wide = own // 256
    chip = 2 * own + (512 if nx <= 2 else 1024)
    shard = 576 // nt
    tall = rows + 4
    few = rows // 2 * half
    vmem = pl.BlockSpec(memory_space=pltpu.VMEM)
    count = (3 * (nx - 1) + 3 * nx + 4 + 2 * levels + (levels - 1) * (nt - 1)
             + levels * (2 * (nt - 1) + ns - 1))
    grad, wg = pl.pallas_call(
        functools.partial(group_kernel, nx, ns, levels),
        out_shape=(
            jax.ShapeDtypeStruct((fl * rows, width), BF),
            jax.ShapeDtypeStruct((levels, nt, shard, 128), BF),
        ),
        in_specs=[vmem] * 7,
        out_specs=(vmem, vmem),
        scratch_shapes=[
            pltpu.VMEM((3, nx, fl, rows, chip + 1024), BF),
            pltpu.VMEM((3, nx, fl, rows, span), BF),
            pltpu.VMEM((2, frames, span), BF),
            pltpu.VMEM((2, frames, span), BF),
            pltpu.VMEM((2, frames, own + 256), BF),
            pltpu.VMEM((2, frames, own + 256), BF),
            pltpu.VMEM((levels, 2, 2 * half, span), BF),
            pltpu.VMEM((levels, 2, 2 * half, span), BF),
            pltpu.VMEM((tall, frames, lanes), F32),
            pltpu.VMEM((tall, frames, lanes), F32),
            pltpu.VMEM((tall, frames, lanes), F32),
            pltpu.VMEM((tall, frames, lanes), F32),
            pltpu.VMEM((rows + 2, frames, lanes), F32),
            pltpu.VMEM((rows + 2, 8, lanes), F32),
            pltpu.VMEM((rows, 8, lanes), F32),
            pltpu.VMEM((tall, 8 * (quads - 2), 512), BF),
            pltpu.VMEM((2, 2, rows + 2, 8 * wide, 512), BF),
            pltpu.VMEM(((rows + 2) // 2 * 8 * (quads - 2), 256), F32),
            pltpu.VMEM((rows * half, own), BF),
            pltpu.VMEM((nt, rows * half, own), BF),
            pltpu.VMEM((2, rows, 8 * wide, 256), BF),
            pltpu.VMEM((2, levels, 3, 512, 256), BF),
            pltpu.VMEM((320, 64), BF),
            pltpu.VMEM((rows * frames, rows * frames), BF),
            pltpu.VMEM((levels, few, few), BF),
            pltpu.VMEM((rows * half, rows * half), BF),
            pltpu.VMEM((fl * rows, rows * half), BF),
            pltpu.VMEM((levels, nt, shard, 128), F32),
            pltpu.VMEM((levels, nt, shard, 128), BF),
            pltpu.VMEM((levels, nt, shard, 128), BF),
            pltpu.VMEM((levels, shard, 128), BF),
            pltpu.VMEM((levels, ns, shard, 128), BF),
            pltpu.VMEM((levels, nt, shard, 128), BF),
            pltpu.SemaphoreType.DMA((count,)),
            pltpu.SemaphoreType.DMA((count,)),
        ],
        compiler_params=pltpu.CompilerParams(
            collective_id=3, has_side_effects=True, vmem_limit_bytes=60 * 2**20
        ),
        name="group",
    )(cotangent, saved_pre, saved_mix, frame_level.reshape(1, frames), ref_pairs,
      kernel_one.reshape(levels, 3, 192, 64), kernel_two.reshape(levels, 3, 192, 64))
    both = wg.reshape(levels, 576, 128).astype(F32)
    one = both[:, :, :64].reshape(kernel_one.shape)
    two = both[:, :, 64:].reshape(kernel_one.shape)
    return (grad.reshape(cotangent.shape).astype(F32), one, two)


def solution(mesh):
    placed = (
        P("tm", "space", None),
        P("tm", "space", None),
        P("tm", "space", None),
        P(),
        P(),
        P(),
        P(),
    )
    return jax.shard_map(
        on_device,
        mesh=mesh,
        in_specs=placed,
        out_specs=(P("tm", "space", None), P(), P()),
        check_vma=False,
    )
```

```python
import functools
import math

import jax
import jax.numpy as jnp
from jax import lax
from jax.experimental import pallas as pl
from jax.experimental.pallas import tpu as pltpu
from jax.sharding import PartitionSpec as P

BF = jnp.bfloat16
F32 = jnp.float32
I32 = jnp.int32


def div(value, n):
    return lax.shift_right_logical(value, jnp.full_like(value, n.bit_length() - 1))


def mod(value, n):
    return jnp.bitwise_and(value, n - 1)


def iota(shape, dim):
    return lax.broadcasted_iota(I32, shape, dim)


def nt_dot(a, b):
    return lax.dot_general(a, b, (((1,), (1,)), ((), ())), preferred_element_type=F32)


def nn_dot(a, b):
    return jnp.dot(a, b, preferred_element_type=F32)


def segments(levels):
    segs = []
    low = 0
    for level in range(levels - 1, 1, -1):
        count = 2 ** (level - 1)
        segs.append((low, count))
        low += count
    segs.append((low, 2))
    return segs


def group_kernel(nx, ns, levels, cot_ref, pre_ref, mix_ref, lev_ref, pairs_ref, k1_ref, k2_ref,
                 grad_ref, wg_ref, rawx, raws, pre_s, pre_r, mix_s, mix_r, cot, pre,
                 mix, act, slope, work, refs, im, imw, imc, conv_out, out_r, rhs_buf, bands, kpad,
                 perm, comb, sel, back, part, ab_s, ab_r, rs_s, rs_r, ag_b, flat_f, ssem, rsem,
                 *halos):
    tm = lax.axis_index("tm")
    sp = lax.axis_index("space")
    xi = tm // 2
    core = tm % 2
    nt = 2 * nx
    fl, rows, width = cot_ref.shape
    frames = fl * nt
    half = frames // 2
    lanes = cot.shape[2]
    own = lanes - 1536
    span = own + 1024
    mid = slice(256, 256 + span)
    quads = lanes // 256
    inner_q = quads - 2
    wide = own // 256
    shard = part.shape[2]
    piece = ag_b.shape[3]
    hal_s, hal_r = halos[:levels], halos[levels:]
    down = (sp + 1) % ns
    up = (sp + ns - 1) % ns
    sib = (xi * 2 + 1 - core, sp)
    chip = rawx.shape[4] - 1024
    tms = [((tm + d) % nt, sp) for d in range(1, nt)]
    xs = [(((xi + d) % nx) * 2 + core, sp) for d in range(1, nx)]
    sps = [(tm, (sp + d) % ns) for d in range(1, ns)]

    barrier = pltpu.get_barrier_semaphore()
    for peer in tms + sps:
        pl.semaphore_signal(barrier, inc=1, device_id=peer, device_id_type=pl.DeviceIdType.MESH)
    slots = [0]

    def send(src, dst, peer):
        copy = pltpu.make_async_remote_copy(
            src_ref=src, dst_ref=dst, send_sem=ssem.at[slots[0]], recv_sem=rsem.at[slots[0]],
            device_id=peer, device_id_type=pl.DeviceIdType.MESH)
        copy.start()
        slots[0] += 1
        return copy

    sources = (cot_ref, pre_ref, mix_ref)
    targets = (cot, pre, mix)

    def chip_start(x):
        start = 2 * own * x - 512 * ((x + nx - 1) // nx)
        if nx > 2:
            start = start - 512 * (x // (nx - 1))
        return start

    def window(x, c):
        return pl.ds(pl.multiple_of((2 * x + c) * own - chip_start(x), 128), span)

    def send_chips(n):
        copies = []
        for d in range(1, nx):
            x = (xi + d) % nx
            cut = pl.ds(pl.multiple_of(chip_start(x), 128), chip)
            copies.append(send(sources[n].at[:, :, cut], rawx.at[n, xi, :, :, 512 : 512 + chip],
                               (x * 2 + core, sp)))
        return copies

    def keep_own(n):
        cut = pl.ds(pl.multiple_of(chip_start(xi), 128), chip)
        rawx[n, xi, :, :, 512 : 512 + chip] = sources[n][:, :, cut]

    def pass_on(n, x):
        return send(rawx.at[n, x, :, :, window(xi, 1 - core)], raws.at[n, x], sib)

    pl.semaphore_wait(barrier, len(tms) + len(sps))
    across = [send_chips(0)]
    rawx[:, :, :, :, 0:512] = jnp.zeros((3, nx, fl, rows, 512), BF)
    rawx[:, :, :, :, 512 + chip :] = jnp.zeros((3, nx, fl, rows, 512), BF)
    passed = [[], [], []]
    for n in range(2):
        keep_own(n)
        passed[n].append(pass_on(n, xi))
    for held in (cot, pre, mix, act):
        held[:, :, 0:256] = jnp.zeros((rows + 4, frames, 256), F32)
        held[:, :, lanes - 256 :] = jnp.zeros((rows + 4, frames, 256), F32)
    for r in (0, 1, rows + 2, rows + 3):
        cot[r] = jnp.zeros((frames, lanes), F32)
    work[...] = jnp.zeros_like(work)

    order_row = (levels - lev_ref[...]) * frames + iota((1, frames), 1)
    order_row = order_row.astype(F32)
    eye = iota((frames, frames), 0) == iota((frames, frames), 1)
    order_col = jnp.sum(jnp.where(eye, jnp.broadcast_to(order_row, (frames, frames)), 0.0),
                        axis=1, keepdims=True)
    rank_row = jnp.sum((order_col < order_row).astype(F32), axis=0, keepdims=True)
    hot = (iota((frames, frames), 0).astype(F32) == rank_row).astype(F32)
    total = frames * rows
    m_id = iota((total, frames), 0)
    to_slot = (mod(m_id, frames) == iota((total, frames), 1)).astype(F32)
    n_id = iota((frames, total), 1)
    side = div(n_id, rows * fl * nx)
    from_core = core + side - 2 * core * side
    from_frame = ((mod(div(n_id, rows * fl), nx) * 2 + from_core) * fl + mod(div(n_id, rows), fl))
    from_hot = (from_frame == iota((frames, total), 0)).astype(F32)
    same_row = div(iota((total, total), 0), frames) == mod(iota((total, total), 1), rows)
    perm[...] = jnp.where(same_row, nn_dot(to_slot, nn_dot(hot, from_hot)), 0.0).astype(BF)
    pairs = pairs_ref[...]
    ref_hot = 0.5 * ((pairs[0:1] == iota((frames, frames), 0)).astype(F32)
                     + (pairs[1:2] == iota((frames, frames), 0)).astype(F32))
    mixw = nt_dot(nn_dot(hot, ref_hot), hot)
    few = rows // 2 * half
    to_low = (mod(iota((few, frames), 0), half) + half == iota((few, frames), 1)).astype(F32)
    same_few = div(iota((few, few), 0), half) == div(iota((few, few), 1), half)
    for k in range(levels):
        g = 0 if k == levels - 1 else half
        lowest = frames - 2 ** (k + 1)
        s_id = mod(iota((frames, few), 1), half) + g
        on = jnp.logical_and(s_id >= lowest, s_id < lowest + 2**k)
        pick = jnp.logical_and(s_id == iota((frames, few), 0), on).astype(F32)
        comb[k] = jnp.where(same_few, nn_dot(nn_dot(to_low, mixw), pick), 0.0).astype(BF)
    low_rows = rows * half
    local = (div(iota((fl * rows, frames), 0), rows) + tm * fl
             == iota((fl * rows, frames), 1)).astype(F32)
    local_hot = nt_dot(local, hot)
    top = jnp.sum(jnp.where(iota((fl * rows, frames), 1) < half, local_hot, 0.0),
                  axis=1, keepdims=True)
    segs = segments(levels)
    o_id = iota((frames, low_rows), 1)
    o_row = mod(iota((fl * rows, low_rows), 0), rows)
    p_id = iota((fl * rows, low_rows), 1)
    slot_of = jnp.zeros_like(o_id)
    row_of = jnp.zeros_like(p_id)
    for low, count in segs:
        here = o_id >= low * rows
        slot_of = jnp.where(here, half + low + mod(o_id - low * rows, count), slot_of)
        there = p_id >= low * rows
        row_of = jnp.where(there, div(p_id - low * rows, count), row_of)
    back[...] = jnp.where(o_row == row_of, nn_dot(
        local_hot, (slot_of == iota((frames, low_rows), 0)).astype(F32)), 0.0).astype(BF)
    for low, count in segs:
        size = rows * count
        a_id = iota((size, low_rows), 0)
        b_id = iota((size, low_rows), 1)
        sel[low * rows : low * rows + size] = jnp.logical_and(
            div(a_id, count) == div(b_id, half),
            low + mod(a_id, count) == mod(b_id, half)).astype(F32).astype(BF)

    for copy in across[0]:
        copy.wait_send()
    across.append(send_chips(1))

    bands[...] = jnp.zeros_like(bands)
    kpad[0:64] = jnp.zeros((64, 64), BF)
    kpad[256:320] = jnp.zeros((64, 64), BF)
    unit = (iota((64, 64), 0) == iota((64, 64), 1)).astype(F32).astype(BF)
    for n in range(2):
        for k in range(levels):
            for a in range(3):
                kpad[64:256] = (k2_ref, k1_ref)[n][k, 2 - a]
                even = nt_dot(unit, kpad[64:320]).astype(BF)
                odd = nt_dot(unit, kpad[0:256]).astype(BF)
                bands[n, k, a, 64:128, 0:128] = even[:, 128:256]
                bands[n, k, a, 128:192, 0:128] = odd[:, 128:256]
                bands[n, k, a, 192:256] = even
                bands[n, k, a, 256:320] = odd
                bands[n, k, a, 320:384, 128:256] = even[:, 0:128]
                bands[n, k, a, 384:448, 128:256] = odd[:, 0:128]

    def gather(n):
        for i, copy in enumerate(across[n]):
            if n == 0:
                copy.wait_recv()
            else:
                copy.wait()
            passed[n].append(pass_on(n, (xi + nx - 1 - i) % nx))
        for copy in passed[n]:
            copy.wait()
        mine = (2 * xi + core) * own - chip_start(xi)
        for j in range(inner_q):
            cut = pl.ds(pl.multiple_of(mine + 256 * j, 128), 256)
            one = rawx[n, :, :, :, cut].astype(F32).reshape(total // 2, 256)
            two = raws[n, :, :, :, 256 * j : 256 * j + 256].astype(F32).reshape(total // 2, 256)
            block = jnp.concatenate((one, two), axis=0).astype(BF)
            moved = nn_dot(perm[...], block)
            targets[n][2 : 2 + rows, :, 256 * j + 256 : 256 * j + 512] = moved.reshape(
                rows, frames, 256)

    def reach(k):
        low = frames - 2 ** (k + 1)
        return slice(low, low + 2**k), slice(768 - 128 * (k + 1), 768 + own + 128 * (k + 1))

    def push(k):
        held, cut = reach(k)
        shape = hal_s[k].shape[1:]
        hal_s[k][0] = cot[2:4, held, cut].reshape(shape).astype(BF)
        hal_s[k][1] = cot[rows : rows + 2, held, cut].reshape(shape).astype(BF)
        return [send(hal_s[k].at[0], hal_r[k].at[1], (tm, up)),
                send(hal_s[k].at[1], hal_r[k].at[0], (tm, down))]

    def land(k, flight):
        for copy in flight:
            copy.wait()
        held, cut = reach(k)
        shape = (2, 2**k, hal_s[k].shape[2])
        cot[0:2, held, cut] = hal_r[k][0].astype(F32).reshape(shape) * has_up
        cot[rows + 2 : rows + 4, held, cut] = hal_r[k][1].astype(F32).reshape(shape) * has_down

    has_up = (sp > 0).astype(F32)
    has_down = (sp < ns - 1).astype(F32)
    column = iota((8, lanes), 1) + tm * own - 768
    inside = jnp.logical_and(column >= 0, column < own * nt).astype(F32)

    gather(0)
    flight = push(levels - 1)
    gather(1)
    across.append(send_chips(2))
    keep_own(2)
    passed[2].append(pass_on(2, xi))
    pre_s[0] = pre[2, :, mid].astype(BF)
    pre_s[1] = pre[rows + 1, :, mid].astype(BF)
    edges = [send(pre_s.at[0], pre_r.at[1], (tm, up)), send(pre_s.at[1], pre_r.at[0], (tm, down))]

    def activate(r):
        gate = has_up if r == 0 else (has_down if r == rows + 1 else 1.0)
        for g in range(0, frames, 8):
            v = pre[r + 1, g : g + 8, mid]
            sig = jax.nn.sigmoid(v)
            slope[r, g : g + 8, mid] = sig * (1.0 + v * (1.0 - sig)) * inside[:, mid] * gate
            act[r + 1, g : g + 8, mid] = v * sig

    def fill(dest, source, g, first, spans, base, width):
        for low, count in spans:
            for r in range(low, low + count):
                for j in range(0, width, 2):
                    lo = 256 * (base + j) - 128
                    one = source[first + r, g : g + 8, lo : lo + 512]
                    two = source[first + r, g : g + 8, lo + 256 : lo + 768]
                    dest[r, 8 * j : 8 * j + 16] = jnp.concatenate((one, two), axis=0).astype(BF)

    def conv(source, n, k, spans, base, width, store):
        total = None
        for a in range(3):
            lhs = [source[low + a : low + a + count, 0 : 8 * width].reshape(count * 8 * width, 512)
                   for low, count in spans]
            lhs = lhs[0] if len(lhs) == 1 else jnp.concatenate(lhs, axis=0)
            term = nn_dot(lhs, bands[n, k, a])
            total = term if total is None else total + term
        conv_out[0 : total.shape[0]] = total
        at = 0
        for low, count in spans:
            for r in range(low, low + count):
                for j in range(width):
                    store(r, base + j, conv_out[at : at + 8])
                    at += 8

    slot_no = iota((8, 256), 0) + 8

    tall = 8 * wide

    def keep_pair(k):
        g = 0 if k == levels - 1 else half
        lowest = frames - 2 ** (k + 1)
        active = jnp.logical_and(slot_no >= lowest, slot_no < lowest + 2**k)
        for n in range(2):
            for r in range(rows):
                for j in range(0, wide, 2):
                    cut = 768 + 256 * j
                    if n == 0:
                        left = work[1 + r, :, cut : cut + 256]
                        right = work[1 + r, :, cut + 256 : cut + 512]
                    else:
                        left = cot[2 + r, g : g + 8, cut : cut + 256]
                        right = cot[2 + r, g : g + 8, cut + 256 : cut + 512]
                    if g:
                        left = jnp.where(active, left, 0.0)
                        right = jnp.where(active, right, 0.0)
                    rhs_buf[k, n, r, 8 * j : 8 * j + 16] = jnp.concatenate(
                        (left, right), axis=0).astype(BF)

    def correlate(k):
        step = math.gcd(192, shard)
        for a in range(3):
            both = []
            for n in range(2):
                rhs = rhs_buf[k, n].reshape(rows * tall, 256)
                lhs = imc[n, 0 if k == levels - 1 else 1, a : a + rows].reshape(rows * tall, 512)
                block = lax.dot_general(
                    lhs, rhs, (((0,), (0,)), ((), ())), preferred_element_type=F32)
                taps = block[64:256, 0:64]
                for p in range(1, 4):
                    taps = taps + block[64 * (p + 1) : 64 * (p + 4), 64 * p : 64 * p + 64]
                both.append(taps)
            joint = jnp.concatenate(both, axis=1) * (1.0 / math.sqrt(rows * ns * (own * nt // 64)))
            for i in range(0, 192, step):
                at = 192 * a + i
                part[k, at // shard, at % shard : at % shard + step] = joint[i : i + step]
        for t in range(nt):
            ab_s[k, t] = part[k, t].astype(BF)
        stage[k] = [send(ab_s.at[k, peer[0]], ab_r.at[k, tm], peer) for peer in tms]

    def arrive(k):
        for copy in stage[k]:
            copy.wait()

    def scatter(k):
        arrive(k)
        value = part[k, tm]
        for d in range(1, nt):
            value = value + ab_r[k, (tm + d) % nt].astype(F32)
        flat_f[0:shard] = value
        for i in range(ns):
            rs_s[k, i] = flat_f[piece * i : piece * i + piece].astype(BF)
        stage[k] = [send(rs_s.at[k, peer[1]], rs_r.at[k, sp], peer) for peer in sps]

    def spread(k):
        arrive(k)
        value = rs_s[k, sp].astype(F32)
        for d in range(1, ns):
            value = value + rs_r[k, (sp + d) % ns].astype(F32)
        ag_b[k, tm, sp] = value.astype(BF)
        stage[k] = [send(ag_b.at[k, tm, sp], ag_b.at[k, tm, sp], peer) for peer in sps]

    def share(k):
        arrive(k)
        stage[k] = [send(ag_b.at[k, tm], ag_b.at[k, tm], peer) for peer in tms]

    def finish(k):
        arrive(k)
        for t in range(nt):
            for i in range(ns):
                flat_f[piece * i : piece * i + piece] = ag_b[k, t, i].astype(F32)
            wg_ref[k, t] = flat_f[0:shard].astype(BF)

    def hand_out(low, count):
        a, b = low * rows, (low + count) * rows
        for j in range(wide):
            cut = slice(768 + 256 * j, 1024 + 256 * j)
            flat = cot[2 : 2 + rows, half:, cut].reshape(low_rows, 256).astype(BF)
            out_r[tm, a:b, 256 * j : 256 * j + 256] = nn_dot(sel[a:b], flat).astype(BF)
        return [send(out_r.at[tm, a:b], out_r.at[tm, a:b], peer) for peer in xs + [sib]]

    def hand_on(low, count, copies):
        a, b = low * rows, (low + count) * rows
        later = copies[-1:]
        for i, copy in enumerate(copies[:-1]):
            copy.wait()
            source = ((xi + nx - 1 - i) % nx) * 2 + core
            later.append(send(out_r.at[source, a:b], out_r.at[source, a:b], sib))
        return later

    stage = {}
    quarter = rows // 4
    inner_one = [(2, rows - 2)]
    outer_one = [(0, 2), (rows, 2)]
    inner_two = [(quarter, rows - 2 * quarter)]
    outer_two = [(0, quarter), (rows - quarter, quarter)]

    def tile(k):
        return 0 if k == levels - 1 else half

    def put_grad(k):
        g = tile(k)

        def store(r, j, block):
            cut = slice(256 * j, 256 * j + 256)
            work[r, :, cut] = (block * slope[r, g : g + 8, cut]).astype(BF).astype(F32)

        return store

    def put_refs(r, j, block):
        cut = slice(256 * j, 256 * j + 256)
        refs[r, :, cut] = block * inside[:, cut]

    def combine(k, spans, base, width):
        for j in range(base, base + width):
            cut = slice(256 * j, 256 * j + 256)
            block = jnp.concatenate([refs[low : low + count, :, cut].reshape(count * 8, 256)
                                     for low, count in spans], axis=0).astype(BF)
            extra = nn_dot(comb[k], block)
            at = 0
            for low, count in spans:
                cot[2 + low : 2 + low + count, half:, cut] += extra[
                    at : at + count * half].reshape(count, half, 256)
                at += count * half

    def bounds(k, n):
        skip = 2 - -(-(2 * k + 1 - n) // 4)
        return 1 + skip, inner_q - 2 * skip

    def first(k, cells, landed):
        base, width = bounds(k, 0)
        fill(im, cot, tile(k), 0, landed, base, width)
        conv(im, 0, k, cells, base, width, put_grad(k))

    def second(k, cells, landed):
        base, width = bounds(k, 1)
        fill(imw, work, 0, 0, landed, base, width)
        conv(imw, 1, k, cells, base, width, put_refs)
        combine(k, cells, base, width)

    top_level = levels - 1
    for r in range(1, rows + 1):
        activate(r)
    first(top_level, inner_one, [(2, rows)])
    for copy in edges:
        copy.wait()
    pre[1, :, mid] = pre_r[0].astype(F32) * has_up
    pre[rows + 2, :, mid] = pre_r[1].astype(F32) * has_down
    activate(0)
    activate(rows + 1)
    moving = []
    for k in range(top_level, -1, -1):
        land(k, flight)
        first(k, outer_one, [(0, 2), (rows + 2, 2)])
        if k == 0:
            keep_pair(0)
            correlate(0)
            scatter(1)
        second(k, outer_two, [(0, rows + 2)])
        if k > 0:
            flight = push(k - 1)
        if k == 1:
            scatter(3)
            scatter(2)
        second(k, inner_two, [])
        if k > 0:
            keep_pair(k)
            first(k - 1, inner_one, [(2, rows)])
        if k == 3:
            fill(imc.at[1, 0], act, 0, 1, [(0, rows + 2)], 3, wide)
            fill(imc.at[1, 1], act, half, 1, [(0, rows + 2)], 3, wide)
            moving.append((segs[0], hand_out(*segs[0])))
            gather(2)
            trim = slice(640, 896 + own)
            mix_s[0] = mix[2, :, trim].astype(BF)
            mix_s[1] = mix[rows + 1, :, trim].astype(BF)
            edges = [send(mix_s.at[0], mix_r.at[1], (tm, up)),
                     send(mix_s.at[1], mix_r.at[0], (tm, down))]
        if k == 2:
            moving.append((segs[1], hand_out(*segs[1])))
            moving[0] = (segs[0], hand_on(*moving[0][0], moving[0][1]))
            for copy in edges:
                copy.wait()
            mix[1, :, trim] = mix_r[0].astype(F32) * has_up
            mix[rows + 2, :, trim] = mix_r[1].astype(F32) * has_down
            fill(imc.at[0, 0], mix, 0, 1, [(0, rows + 2)], 3, wide)
            fill(imc.at[0, 1], mix, half, 1, [(0, rows + 2)], 3, wide)
            correlate(3)
            correlate(2)
        if k == 1:
            moving[1] = (segs[1], hand_on(*moving[1][0], moving[1][1]))
            correlate(1)
            spread(3)
            spread(2)
    moving.append((segs[2], hand_out(*segs[2])))
    scatter(0)
    spread(1)
    share(3)
    share(2)
    moving[2] = (segs[2], hand_on(*moving[2][0], moving[2][1]))
    spread(0)
    share(1)
    finish(3)
    finish(2)
    for _, copies in moving:
        for copy in copies:
            copy.wait()
    for t in range(nt):
        for j in range(wide):
            cut = slice(own * t + 256 * j, own * t + 256 * j + 256)
            plain = cot_ref[:, :, cut].astype(F32).reshape(fl * rows, 256)
            value = nn_dot(back[...], out_r[t, :, 256 * j : 256 * j + 256]) + top * plain
            grad_ref[:, cut] = value.astype(BF)
    share(0)
    finish(1)
    finish(0)


def on_device(cotangent, saved_mix, saved_pre, kernel_one, kernel_two, ref_pairs, frame_level):
    fl, rows, width = cotangent.shape
    nt = lax.axis_size("tm")
    nx = nt // 2
    ns = lax.axis_size("space")
    levels = kernel_one.shape[0]
    frames = fl * nt
    half = frames // 2
    own = width // nt
    lanes = own + 1536
    span = own + 1024
    quads = lanes // 256
    wide = own // 256
    chip = 2 * own + (512 if nx <= 2 else 1024)
    shard = 576 // nt
    tall = rows + 4
    few = rows // 2 * half
    vmem = pl.BlockSpec(memory_space=pltpu.VMEM)
    piece = -(-shard // ns)
    count = (3 * (nx - 1) + 3 * nx + 4 + 2 * levels + (levels - 1) * (2 * nx - 1)
             + 2 * levels * (nt - 1 + ns - 1))
    halo = [pltpu.VMEM((2, 2 * 2**k, own + 256 * (k + 1)), BF) for k in range(levels)]
    grad, wg = pl.pallas_call(
        functools.partial(group_kernel, nx, ns, levels),
        out_shape=(
            jax.ShapeDtypeStruct((fl * rows, width), BF),
            jax.ShapeDtypeStruct((levels, nt, shard, 128), BF),
        ),
        in_specs=[vmem] * 7,
        out_specs=(vmem, vmem),
        scratch_shapes=[
            pltpu.VMEM((3, nx, fl, rows, chip + 1024), BF),
            pltpu.VMEM((3, nx, fl, rows, span), BF),
            pltpu.VMEM((2, frames, span), BF),
            pltpu.VMEM((2, frames, span), BF),
            pltpu.VMEM((2, frames, own + 256), BF),
            pltpu.VMEM((2, frames, own + 256), BF),
            pltpu.VMEM((tall, frames, lanes), F32),
            pltpu.VMEM((tall, frames, lanes), F32),
            pltpu.VMEM((tall, frames, lanes), F32),
            pltpu.VMEM((tall, frames, lanes), F32),
            pltpu.VMEM((rows + 2, frames, lanes), F32),
            pltpu.VMEM((rows + 2, 8, lanes), F32),
            pltpu.VMEM((rows, 8, lanes), F32),
            pltpu.VMEM((tall, 8 * (quads - 2), 512), BF),
            pltpu.VMEM((rows + 2, 8 * (quads - 2), 512), BF),
            pltpu.VMEM((2, 2, rows + 2, 8 * wide, 512), BF),
            pltpu.VMEM(((rows - 2) * 8 * (quads - 2), 256), F32),
            pltpu.VMEM((nt, rows * half, own), BF),
            pltpu.VMEM((levels, 2, rows, 8 * wide, 256), BF),
            pltpu.VMEM((2, levels, 3, 512, 256), BF),
            pltpu.VMEM((320, 64), BF),
            pltpu.VMEM((rows * frames, rows * frames), BF),
            pltpu.VMEM((levels, few, few), BF),
            pltpu.VMEM((rows * half, rows * half), BF),
            pltpu.VMEM((fl * rows, rows * half), BF),
            pltpu.VMEM((levels, nt, shard, 128), F32),
            pltpu.VMEM((levels, nt, shard, 128), BF),
            pltpu.VMEM((levels, nt, shard, 128), BF),
            pltpu.VMEM((levels, ns, piece, 128), BF),
            pltpu.VMEM((levels, ns, piece, 128), BF),
            pltpu.VMEM((levels, nt, ns, piece, 128), BF),
            pltpu.VMEM((ns * piece, 128), F32),
            pltpu.SemaphoreType.DMA((count,)),
            pltpu.SemaphoreType.DMA((count,)),
        ] + halo + halo,
        compiler_params=pltpu.CompilerParams(
            collective_id=3, has_side_effects=True, vmem_limit_bytes=60 * 2**20
        ),
        name="group",
    )(cotangent, saved_pre, saved_mix, frame_level.reshape(1, frames), ref_pairs.T,
      kernel_one.reshape(levels, 3, 192, 64), kernel_two.reshape(levels, 3, 192, 64))
    both = wg.reshape(levels, 576, 128).astype(F32)
    one = both[:, :, :64].reshape(kernel_one.shape)
    two = both[:, :, 64:].reshape(kernel_one.shape)
    return (grad.reshape(cotangent.shape).astype(F32), one, two)


def solution(mesh):
    placed = (
        P("tm", "space", None),
        P("tm", "space", None),
        P("tm", "space", None),
        P(),
        P(),
        P(),
        P(),
    )
    return jax.shard_map(
        on_device,
        mesh=mesh,
        in_specs=placed,
        out_specs=(P("tm", "space", None), P(), P()),
        check_vma=False,
    )
```

```python
import functools
import math

import jax
import jax.numpy as jnp
from jax import lax
from jax.experimental import pallas as pl
from jax.experimental.pallas import tpu as pltpu
from jax.sharding import PartitionSpec as P

BF = jnp.bfloat16
F32 = jnp.float32
I32 = jnp.int32


def div(value, n):
    return lax.shift_right_logical(value, jnp.full_like(value, n.bit_length() - 1))


def mod(value, n):
    return jnp.bitwise_and(value, n - 1)


def iota(shape, dim):
    return lax.broadcasted_iota(I32, shape, dim)


def nt_dot(a, b):
    return lax.dot_general(a, b, (((1,), (1,)), ((), ())), preferred_element_type=F32)


def nn_dot(a, b):
    return jnp.dot(a, b, preferred_element_type=F32)


def segments(levels):
    segs = []
    low = 0
    for level in range(levels - 1, 1, -1):
        count = 2 ** (level - 1)
        segs.append((low, count))
        low += count
    segs.append((low, 2))
    return segs


def group_kernel(nx, ns, levels, cot_ref, pre_ref, mix_ref, lev_ref, pairs_ref, k1_hbm, k2_hbm,
                 grad_ref, wg_ref, rawx, raws, pre_s, pre_r, mix_s, mix_r, cot, pre,
                 mix, act, slope, work, refs, im, imw, imc, conv_out, out_r, rhs_buf, bands, kpad,
                 perm, comb, sel, back, part, ab_s, ab_r, rs_s, rs_r, ag_b, flat_f, whole, k1_ref, k2_ref,
                 lsem, ssem, rsem,
                 *halos):
    tm = lax.axis_index("tm")
    sp = lax.axis_index("space")
    xi = tm // 2
    core = tm % 2
    nt = 2 * nx
    fl, rows, width = cot_ref.shape
    frames = fl * nt
    half = frames // 2
    lanes = cot.shape[2]
    own = lanes - 1536
    span = own + 1024
    mid = slice(256, 256 + span)
    quads = lanes // 256
    inner_q = quads - 2
    wide = own // 256
    shard = part.shape[2]
    piece = ag_b.shape[3]
    hal_s, hal_r = halos[:levels], halos[levels:]
    down = (sp + 1) % ns
    up = (sp + ns - 1) % ns
    sib = (xi * 2 + 1 - core, sp)
    chip = rawx.shape[4] - 1024
    tms = [((tm + d) % nt, sp) for d in range(1, nt)]
    xs = [(((xi + d) % nx) * 2 + core, sp) for d in range(1, nx)]
    sps = [(tm, (sp + d) % ns) for d in range(1, ns)]

    barrier = pltpu.get_barrier_semaphore()
    for peer in tms + sps:
        pl.semaphore_signal(barrier, inc=1, device_id=peer, device_id_type=pl.DeviceIdType.MESH)
    slots = [0]

    def send(src, dst, peer):
        copy = pltpu.make_async_remote_copy(
            src_ref=src, dst_ref=dst, send_sem=ssem.at[slots[0]], recv_sem=rsem.at[slots[0]],
            device_id=peer, device_id_type=pl.DeviceIdType.MESH)
        copy.start()
        slots[0] += 1
        return copy

    sources = (cot_ref, pre_ref, mix_ref)
    targets = (cot, pre, mix)

    def chip_start(x):
        start = 2 * own * x - 512 * ((x + nx - 1) // nx)
        if nx > 2:
            start = start - 512 * (x // (nx - 1))
        return start

    def window(x, c):
        return pl.ds(pl.multiple_of((2 * x + c) * own - chip_start(x), 128), span)

    def send_chips(n):
        copies = []
        for d in range(1, nx):
            x = (xi + d) % nx
            cut = pl.ds(pl.multiple_of(chip_start(x), 128), chip)
            copies.append(send(sources[n].at[:, :, cut], rawx.at[n, xi, :, :, 512 : 512 + chip],
                               (x * 2 + core, sp)))
        return copies

    mine = pl.ds(pl.multiple_of(chip_start(xi), 128), chip)
    loads = [pltpu.make_async_copy(sources[n].at[:, :, mine],
                                   rawx.at[n, xi, :, :, 512 : 512 + chip], lsem.at[n])
             for n in range(3)]
    loads += [pltpu.make_async_copy(k1_hbm, k1_ref, lsem.at[3]),
              pltpu.make_async_copy(k2_hbm, k2_ref, lsem.at[4]),
              pltpu.make_async_copy(cot_ref, whole, lsem.at[5])]
    for n in (0, 1, 3, 4):
        loads[n].start()

    def pass_on(n, x):
        return send(rawx.at[n, x, :, :, window(xi, 1 - core)], raws.at[n, x], sib)

    pl.semaphore_wait(barrier, len(tms) + len(sps))
    across = [send_chips(0)]
    rawx[:, :, :, :, 0:512] = jnp.zeros((3, nx, fl, rows, 512), BF)
    rawx[:, :, :, :, 512 + chip :] = jnp.zeros((3, nx, fl, rows, 512), BF)
    passed = [[], [], []]
    for n in range(2):
        loads[n].wait()
        passed[n].append(pass_on(n, xi))
    loads[2].start()
    loads[5].start()
    for held in (cot, pre, mix, act):
        held[:, :, 0:256] = jnp.zeros((rows + 4, frames, 256), F32)
        held[:, :, lanes - 256 :] = jnp.zeros((rows + 4, frames, 256), F32)
    for r in (0, 1, rows + 2, rows + 3):
        cot[r] = jnp.zeros((frames, lanes), F32)
    work[...] = jnp.zeros_like(work)

    order_row = (levels - lev_ref[...]) * frames + iota((1, frames), 1)
    order_row = order_row.astype(F32)
    eye = iota((frames, frames), 0) == iota((frames, frames), 1)
    order_col = jnp.sum(jnp.where(eye, jnp.broadcast_to(order_row, (frames, frames)), 0.0),
                        axis=1, keepdims=True)
    rank_row = jnp.sum((order_col < order_row).astype(F32), axis=0, keepdims=True)
    hot = (iota((frames, frames), 0).astype(F32) == rank_row).astype(F32)
    total = frames * rows
    m_id = iota((total, frames), 0)
    to_slot = (mod(m_id, frames) == iota((total, frames), 1)).astype(F32)
    n_id = iota((frames, total), 1)
    side = div(n_id, rows * fl * nx)
    from_core = core + side - 2 * core * side
    from_frame = ((mod(div(n_id, rows * fl), nx) * 2 + from_core) * fl + mod(div(n_id, rows), fl))
    from_hot = (from_frame == iota((frames, total), 0)).astype(F32)
    same_row = div(iota((total, total), 0), frames) == mod(iota((total, total), 1), rows)
    perm[...] = jnp.where(same_row, nn_dot(to_slot, nn_dot(hot, from_hot)), 0.0).astype(BF)
    pairs = pairs_ref[...]
    ref_hot = 0.5 * ((pairs[0:1] == iota((frames, frames), 0)).astype(F32)
                     + (pairs[1:2] == iota((frames, frames), 0)).astype(F32))
    mixw = nt_dot(nn_dot(hot, ref_hot), hot)
    few = rows // 2 * half
    to_low = (mod(iota((few, frames), 0), half) + half == iota((few, frames), 1)).astype(F32)
    same_few = div(iota((few, few), 0), half) == div(iota((few, few), 1), half)
    for k in range(levels):
        g = 0 if k == levels - 1 else half
        lowest = frames - 2 ** (k + 1)
        s_id = mod(iota((frames, few), 1), half) + g
        on = jnp.logical_and(s_id >= lowest, s_id < lowest + 2**k)
        pick = jnp.logical_and(s_id == iota((frames, few), 0), on).astype(F32)
        comb[k] = jnp.where(same_few, nn_dot(nn_dot(to_low, mixw), pick), 0.0).astype(BF)
    low_rows = rows * half
    local = (div(iota((fl * rows, frames), 0), rows) + tm * fl
             == iota((fl * rows, frames), 1)).astype(F32)
    local_hot = nt_dot(local, hot)
    top = jnp.sum(jnp.where(iota((fl * rows, frames), 1) < half, local_hot, 0.0),
                  axis=1, keepdims=True)
    segs = segments(levels)
    o_id = iota((frames, low_rows), 1)
    o_row = mod(iota((fl * rows, low_rows), 0), rows)
    p_id = iota((fl * rows, low_rows), 1)
    slot_of = jnp.zeros_like(o_id)
    row_of = jnp.zeros_like(p_id)
    for low, count in segs:
        here = o_id >= low * rows
        slot_of = jnp.where(here, half + low + mod(o_id - low * rows, count), slot_of)
        there = p_id >= low * rows
        row_of = jnp.where(there, div(p_id - low * rows, count), row_of)
    back[...] = jnp.where(o_row == row_of, nn_dot(
        local_hot, (slot_of == iota((frames, low_rows), 0)).astype(F32)), 0.0).astype(BF)
    for low, count in segs:
        size = rows * count
        a_id = iota((size, low_rows), 0)
        b_id = iota((size, low_rows), 1)
        sel[low * rows : low * rows + size] = jnp.logical_and(
            div(a_id, count) == div(b_id, half),
            low + mod(a_id, count) == mod(b_id, half)).astype(F32).astype(BF)

    for copy in across[0]:
        copy.wait_send()
    across.append(send_chips(1))

    bands[...] = jnp.zeros_like(bands)
    loads[3].wait()
    loads[4].wait()
    kpad[0:64] = jnp.zeros((64, 64), BF)
    kpad[256:320] = jnp.zeros((64, 64), BF)
    unit = (iota((64, 64), 0) == iota((64, 64), 1)).astype(F32).astype(BF)
    for n in range(2):
        for k in range(levels):
            for a in range(3):
                kpad[64:256] = (k2_ref, k1_ref)[n][k, 2 - a]
                even = nt_dot(unit, kpad[64:320]).astype(BF)
                odd = nt_dot(unit, kpad[0:256]).astype(BF)
                bands[n, k, a, 64:128, 0:128] = even[:, 128:256]
                bands[n, k, a, 128:192, 0:128] = odd[:, 128:256]
                bands[n, k, a, 192:256] = even
                bands[n, k, a, 256:320] = odd
                bands[n, k, a, 320:384, 128:256] = even[:, 0:128]
                bands[n, k, a, 384:448, 128:256] = odd[:, 0:128]

    def gather(n):
        for i, copy in enumerate(across[n]):
            if n == 0:
                copy.wait_recv()
            else:
                copy.wait()
            passed[n].append(pass_on(n, (xi + nx - 1 - i) % nx))
        for copy in passed[n]:
            copy.wait()
        mine = (2 * xi + core) * own - chip_start(xi)
        for j in range(inner_q):
            cut = pl.ds(pl.multiple_of(mine + 256 * j, 128), 256)
            one = rawx[n, :, :, :, cut].astype(F32).reshape(total // 2, 256)
            two = raws[n, :, :, :, 256 * j : 256 * j + 256].astype(F32).reshape(total // 2, 256)
            block = jnp.concatenate((one, two), axis=0).astype(BF)
            moved = nn_dot(perm[...], block)
            targets[n][2 : 2 + rows, :, 256 * j + 256 : 256 * j + 512] = moved.reshape(
                rows, frames, 256)

    def reach(k):
        low = frames - 2 ** (k + 1)
        return slice(low, low + 2**k), slice(768 - 128 * (k + 1), 768 + own + 128 * (k + 1))

    def push(k):
        held, cut = reach(k)
        shape = hal_s[k].shape[1:]
        hal_s[k][0] = cot[2:4, held, cut].reshape(shape).astype(BF)
        hal_s[k][1] = cot[rows : rows + 2, held, cut].reshape(shape).astype(BF)
        return [send(hal_s[k].at[0], hal_r[k].at[1], (tm, up)),
                send(hal_s[k].at[1], hal_r[k].at[0], (tm, down))]

    def land(k, flight):
        for copy in flight:
            copy.wait()
        held, cut = reach(k)
        shape = (2, 2**k, hal_s[k].shape[2])
        cot[0:2, held, cut] = hal_r[k][0].astype(F32).reshape(shape) * has_up
        cot[rows + 2 : rows + 4, held, cut] = hal_r[k][1].astype(F32).reshape(shape) * has_down

    has_up = (sp > 0).astype(F32)
    has_down = (sp < ns - 1).astype(F32)
    column = iota((8, lanes), 1) + tm * own - 768
    inside = jnp.logical_and(column >= 0, column < own * nt).astype(F32)

    gather(0)
    flight = push(levels - 1)
    gather(1)
    across.append(send_chips(2))
    loads[2].wait()
    passed[2].append(pass_on(2, xi))
    pre_s[0] = pre[2, :, mid].astype(BF)
    pre_s[1] = pre[rows + 1, :, mid].astype(BF)
    edges = [send(pre_s.at[0], pre_r.at[1], (tm, up)), send(pre_s.at[1], pre_r.at[0], (tm, down))]

    def activate(r):
        gate = has_up if r == 0 else (has_down if r == rows + 1 else 1.0)
        for g in range(0, frames, 8):
            v = pre[r + 1, g : g + 8, mid]
            sig = jax.nn.sigmoid(v)
            slope[r, g : g + 8, mid] = sig * (1.0 + v * (1.0 - sig)) * inside[:, mid] * gate
            act[r + 1, g : g + 8, mid] = v * sig

    def fill(dest, source, g, first, spans, base, width):
        for low, count in spans:
            for r in range(low, low + count):
                for j in range(0, width, 2):
                    lo = 256 * (base + j) - 128
                    one = source[first + r, g : g + 8, lo : lo + 512]
                    two = source[first + r, g : g + 8, lo + 256 : lo + 768]
                    dest[r, 8 * j : 8 * j + 16] = jnp.concatenate((one, two), axis=0).astype(BF)

    def conv(source, n, k, spans, base, width, store):
        total = None
        for a in range(3):
            lhs = [source[low + a : low + a + count, 0 : 8 * width].reshape(count * 8 * width, 512)
                   for low, count in spans]
            lhs = lhs[0] if len(lhs) == 1 else jnp.concatenate(lhs, axis=0)
            term = nn_dot(lhs, bands[n, k, a])
            total = term if total is None else total + term
        conv_out[0 : total.shape[0]] = total
        at = 0
        for low, count in spans:
            for r in range(low, low + count):
                for j in range(width):
                    store(r, base + j, conv_out[at : at + 8])
                    at += 8

    slot_no = iota((8, 256), 0) + 8

    tall = 8 * wide

    def keep_pair(k):
        g = 0 if k == levels - 1 else half
        lowest = frames - 2 ** (k + 1)
        active = jnp.logical_and(slot_no >= lowest, slot_no < lowest + 2**k)
        for n in range(2):
            for r in range(rows):
                for j in range(0, wide, 2):
                    cut = 768 + 256 * j
                    if n == 0:
                        left = work[1 + r, :, cut : cut + 256]
                        right = work[1 + r, :, cut + 256 : cut + 512]
                    else:
                        left = cot[2 + r, g : g + 8, cut : cut + 256]
                        right = cot[2 + r, g : g + 8, cut + 256 : cut + 512]
                    if g:
                        left = jnp.where(active, left, 0.0)
                        right = jnp.where(active, right, 0.0)
                    rhs_buf[k, n, r, 8 * j : 8 * j + 16] = jnp.concatenate(
                        (left, right), axis=0).astype(BF)

    def correlate(k):
        step = math.gcd(192, shard)
        for a in range(3):
            both = []
            for n in range(2):
                rhs = rhs_buf[k, n].reshape(rows * tall, 256)
                lhs = imc[n, 0 if k == levels - 1 else 1, a : a + rows].reshape(rows * tall, 512)
                block = lax.dot_general(
                    lhs, rhs, (((0,), (0,)), ((), ())), preferred_element_type=F32)
                taps = block[64:256, 0:64]
                for p in range(1, 4):
                    taps = taps + block[64 * (p + 1) : 64 * (p + 4), 64 * p : 64 * p + 64]
                both.append(taps)
            joint = jnp.concatenate(both, axis=1) * (1.0 / math.sqrt(rows * ns * (own * nt // 64)))
            for i in range(0, 192, step):
                at = 192 * a + i
                part[k, at // shard, at % shard : at % shard + step] = joint[i : i + step]
        for t in range(nt):
            ab_s[k, t] = part[k, t].astype(BF)
        stage[k] = [send(ab_s.at[k, peer[0]], ab_r.at[k, tm], peer) for peer in tms]

    def arrive(k):
        for copy in stage[k]:
            copy.wait()

    def scatter(k):
        arrive(k)
        value = part[k, tm]
        for d in range(1, nt):
            value = value + ab_r[k, (tm + d) % nt].astype(F32)
        flat_f[0:shard] = value
        for i in range(ns):
            rs_s[k, i] = flat_f[piece * i : piece * i + piece].astype(BF)
        stage[k] = [send(rs_s.at[k, peer[1]], rs_r.at[k, sp], peer) for peer in sps]

    def spread(k):
        arrive(k)
        value = rs_s[k, sp].astype(F32)
        for d in range(1, ns):
            value = value + rs_r[k, (sp + d) % ns].astype(F32)
        ag_b[k, tm, sp] = value.astype(BF)
        stage[k] = [send(ag_b.at[k, tm, sp], ag_b.at[k, tm, sp], peer) for peer in sps]

    def share(k):
        arrive(k)
        stage[k] = [send(ag_b.at[k, tm], ag_b.at[k, tm], peer) for peer in tms]

    def finish(k):
        arrive(k)
        for t in range(nt):
            for i in range(ns):
                flat_f[piece * i : piece * i + piece] = ag_b[k, t, i].astype(F32)
            wg_ref[k, t] = flat_f[0:shard].astype(BF)

    def hand_out(low, count):
        a, b = low * rows, (low + count) * rows
        for j in range(wide):
            cut = slice(768 + 256 * j, 1024 + 256 * j)
            flat = cot[2 : 2 + rows, half:, cut].reshape(low_rows, 256).astype(BF)
            out_r[tm, a:b, 256 * j : 256 * j + 256] = nn_dot(sel[a:b], flat).astype(BF)
        return [send(out_r.at[tm, a:b], out_r.at[tm, a:b], peer) for peer in xs + [sib]]

    def hand_on(low, count, copies):
        a, b = low * rows, (low + count) * rows
        later = copies[-1:]
        for i, copy in enumerate(copies[:-1]):
            copy.wait()
            source = ((xi + nx - 1 - i) % nx) * 2 + core
            later.append(send(out_r.at[source, a:b], out_r.at[source, a:b], sib))
        return later

    stage = {}
    quarter = rows // 4
    inner_one = [(2, rows - 2)]
    outer_one = [(0, 2), (rows, 2)]
    inner_two = [(quarter, rows - 2 * quarter)]
    outer_two = [(0, quarter), (rows - quarter, quarter)]

    def tile(k):
        return 0 if k == levels - 1 else half

    def put_grad(k):
        g = tile(k)

        def store(r, j, block):
            cut = slice(256 * j, 256 * j + 256)
            work[r, :, cut] = (block * slope[r, g : g + 8, cut]).astype(BF).astype(F32)

        return store

    def put_refs(r, j, block):
        cut = slice(256 * j, 256 * j + 256)
        refs[r, :, cut] = block * inside[:, cut]

    def combine(k, spans, base, width):
        for j in range(base, base + width):
            cut = slice(256 * j, 256 * j + 256)
            block = jnp.concatenate([refs[low : low + count, :, cut].reshape(count * 8, 256)
                                     for low, count in spans], axis=0).astype(BF)
            extra = nn_dot(comb[k], block)
            at = 0
            for low, count in spans:
                cot[2 + low : 2 + low + count, half:, cut] += extra[
                    at : at + count * half].reshape(count, half, 256)
                at += count * half

    def bounds(k, n):
        skip = 2 - -(-(2 * k + 1 - n) // 4)
        return 1 + skip, inner_q - 2 * skip

    def first(k, cells, landed):
        base, width = bounds(k, 0)
        fill(im, cot, tile(k), 0, landed, base, width)
        conv(im, 0, k, cells, base, width, put_grad(k))

    def second(k, cells, landed):
        base, width = bounds(k, 1)
        fill(imw, work, 0, 0, landed, base, width)
        conv(imw, 1, k, cells, base, width, put_refs)
        combine(k, cells, base, width)

    top_level = levels - 1
    for r in range(1, rows + 1):
        activate(r)
    first(top_level, inner_one, [(2, rows)])
    for copy in edges:
        copy.wait()
    pre[1, :, mid] = pre_r[0].astype(F32) * has_up
    pre[rows + 2, :, mid] = pre_r[1].astype(F32) * has_down
    activate(0)
    activate(rows + 1)
    moving = []
    for k in range(top_level, -1, -1):
        land(k, flight)
        first(k, outer_one, [(0, 2), (rows + 2, 2)])
        if k == 0:
            keep_pair(0)
            correlate(0)
            scatter(1)
        second(k, outer_two, [(0, rows + 2)])
        if k > 0:
            flight = push(k - 1)
        if k == 1:
            scatter(3)
            scatter(2)
        second(k, inner_two, [])
        if k > 0:
            keep_pair(k)
            first(k - 1, inner_one, [(2, rows)])
        if k == 3:
            fill(imc.at[1, 0], act, 0, 1, [(0, rows + 2)], 3, wide)
            fill(imc.at[1, 1], act, half, 1, [(0, rows + 2)], 3, wide)
            moving.append((segs[0], hand_out(*segs[0])))
            gather(2)
            trim = slice(640, 896 + own)
            mix_s[0] = mix[2, :, trim].astype(BF)
            mix_s[1] = mix[rows + 1, :, trim].astype(BF)
            edges = [send(mix_s.at[0], mix_r.at[1], (tm, up)),
                     send(mix_s.at[1], mix_r.at[0], (tm, down))]
        if k == 2:
            moving.append((segs[1], hand_out(*segs[1])))
            moving[0] = (segs[0], hand_on(*moving[0][0], moving[0][1]))
            for copy in edges:
                copy.wait()
            mix[1, :, trim] = mix_r[0].astype(F32) * has_up
            mix[rows + 2, :, trim] = mix_r[1].astype(F32) * has_down
            fill(imc.at[0, 0], mix, 0, 1, [(0, rows + 2)], 3, wide)
            fill(imc.at[0, 1], mix, half, 1, [(0, rows + 2)], 3, wide)
            correlate(3)
            correlate(2)
        if k == 1:
            moving[1] = (segs[1], hand_on(*moving[1][0], moving[1][1]))
            correlate(1)
            spread(3)
            spread(2)
    moving.append((segs[2], hand_out(*segs[2])))
    scatter(0)
    spread(1)
    share(3)
    share(2)
    moving[2] = (segs[2], hand_on(*moving[2][0], moving[2][1]))
    spread(0)
    share(1)
    loads[5].wait()
    finish(3)
    finish(2)
    for _, copies in moving:
        for copy in copies:
            copy.wait()
    for t in range(nt):
        for j in range(wide):
            cut = slice(own * t + 256 * j, own * t + 256 * j + 256)
            plain = whole[:, :, cut].astype(F32).reshape(fl * rows, 256)
            value = nn_dot(back[...], out_r[t, :, 256 * j : 256 * j + 256]) + top * plain
            grad_ref[:, cut] = value.astype(BF)
    share(0)
    finish(1)
    finish(0)


def widen_kernel(grad_ref, wg_ref, out_ref, one_ref, two_ref):
    out_ref[...] = grad_ref[...].astype(F32)
    one_ref[...] = wg_ref[:, 0:64].astype(F32)
    two_ref[...] = wg_ref[:, 64:128].astype(F32)


def on_device(cotangent, saved_mix, saved_pre, kernel_one, kernel_two, ref_pairs, frame_level):
    fl, rows, width = cotangent.shape
    nt = lax.axis_size("tm")
    nx = nt // 2
    ns = lax.axis_size("space")
    levels = kernel_one.shape[0]
    frames = fl * nt
    half = frames // 2
    own = width // nt
    lanes = own + 1536
    span = own + 1024
    quads = lanes // 256
    wide = own // 256
    chip = 2 * own + (512 if nx <= 2 else 1024)
    shard = 576 // nt
    tall = rows + 4
    few = rows // 2 * half
    vmem = pl.BlockSpec(memory_space=pltpu.VMEM)
    hbm = pl.BlockSpec(memory_space=pl.ANY)
    piece = -(-shard // ns)
    count = (3 * (nx - 1) + 3 * nx + 4 + 2 * levels + (levels - 1) * (2 * nx - 1)
             + 2 * levels * (nt - 1 + ns - 1))
    halo = [pltpu.VMEM((2, 2 * 2**k, own + 256 * (k + 1)), BF) for k in range(levels)]
    grad, wg = pl.pallas_call(
        functools.partial(group_kernel, nx, ns, levels),
        out_shape=(
            jax.ShapeDtypeStruct((fl * rows, width), BF),
            jax.ShapeDtypeStruct((levels, nt, shard, 128), BF),
        ),
        in_specs=[hbm] * 3 + [vmem] * 2 + [hbm] * 2,
        out_specs=(vmem, vmem),
        scratch_shapes=[
            pltpu.VMEM((3, nx, fl, rows, chip + 1024), BF),
            pltpu.VMEM((3, nx, fl, rows, span), BF),
            pltpu.VMEM((2, frames, span), BF),
            pltpu.VMEM((2, frames, span), BF),
            pltpu.VMEM((2, frames, own + 256), BF),
            pltpu.VMEM((2, frames, own + 256), BF),
            pltpu.VMEM((tall, frames, lanes), F32),
            pltpu.VMEM((tall, frames, lanes), F32),
            pltpu.VMEM((tall, frames, lanes), F32),
            pltpu.VMEM((tall, frames, lanes), F32),
            pltpu.VMEM((rows + 2, frames, lanes), F32),
            pltpu.VMEM((rows + 2, 8, lanes), F32),
            pltpu.VMEM((rows, 8, lanes), F32),
            pltpu.VMEM((tall, 8 * (quads - 2), 512), BF),
            pltpu.VMEM((rows + 2, 8 * (quads - 2), 512), BF),
            pltpu.VMEM((2, 2, rows + 2, 8 * wide, 512), BF),
            pltpu.VMEM(((rows - 2) * 8 * (quads - 2), 256), F32),
            pltpu.VMEM((nt, rows * half, own), BF),
            pltpu.VMEM((levels, 2, rows, 8 * wide, 256), BF),
            pltpu.VMEM((2, levels, 3, 512, 256), BF),
            pltpu.VMEM((320, 64), BF),
            pltpu.VMEM((rows * frames, rows * frames), BF),
            pltpu.VMEM((levels, few, few), BF),
            pltpu.VMEM((rows * half, rows * half), BF),
            pltpu.VMEM((fl * rows, rows * half), BF),
            pltpu.VMEM((levels, nt, shard, 128), F32),
            pltpu.VMEM((levels, nt, shard, 128), BF),
            pltpu.VMEM((levels, nt, shard, 128), BF),
            pltpu.VMEM((levels, ns, piece, 128), BF),
            pltpu.VMEM((levels, ns, piece, 128), BF),
            pltpu.VMEM((levels, nt, ns, piece, 128), BF),
            pltpu.VMEM((ns * piece, 128), F32),
            pltpu.VMEM((fl, rows, width), BF),
            pltpu.VMEM((levels, 3, 192, 64), BF),
            pltpu.VMEM((levels, 3, 192, 64), BF),
            pltpu.SemaphoreType.DMA((6,)),
            pltpu.SemaphoreType.DMA((count,)),
            pltpu.SemaphoreType.DMA((count,)),
        ] + halo + halo,
        compiler_params=pltpu.CompilerParams(
            collective_id=3, has_side_effects=True, vmem_limit_bytes=60 * 2**20
        ),
        name="group",
    )(cotangent, saved_pre, saved_mix, frame_level.reshape(1, frames), ref_pairs.T,
      kernel_one.reshape(levels, 3, 192, 64), kernel_two.reshape(levels, 3, 192, 64))
    grad, one, two = pl.pallas_call(
        widen_kernel,
        grid=(levels,),
        out_shape=(
            jax.ShapeDtypeStruct((fl * rows, width), F32),
            jax.ShapeDtypeStruct((levels * 576, 64), F32),
            jax.ShapeDtypeStruct((levels * 576, 64), F32),
        ),
        in_specs=[pl.BlockSpec((fl * rows, width // levels), lambda i: (0, i)),
                  pl.BlockSpec((576, 128), lambda i: (i, 0))],
        out_specs=(pl.BlockSpec((fl * rows, width // levels), lambda i: (0, i)),
                   pl.BlockSpec((576, 64), lambda i: (i, 0)),
                   pl.BlockSpec((576, 64), lambda i: (i, 0))),
        name="widen",
    )(grad, wg.reshape(levels * 576, 128))
    return (grad.reshape(cotangent.shape), one.reshape(kernel_one.shape),
            two.reshape(kernel_one.shape))


def solution(mesh):
    placed = (
        P("tm", "space", None),
        P("tm", "space", None),
        P("tm", "space", None),
        P(),
        P(),
        P(),
        P(),
    )
    return jax.shard_map(
        on_device,
        mesh=mesh,
        in_specs=placed,
        out_specs=(P("tm", "space", None), P(), P()),
        check_vma=False,
    )
```

```python
import functools
import math

import jax
import jax.numpy as jnp
from jax import lax
from jax.experimental import pallas as pl
from jax.experimental.pallas import tpu as pltpu
from jax.sharding import PartitionSpec as P

BF = jnp.bfloat16
F32 = jnp.float32
I32 = jnp.int32


def div(value, n):
    return lax.shift_right_logical(value, jnp.full_like(value, n.bit_length() - 1))


def mod(value, n):
    return jnp.bitwise_and(value, n - 1)


def iota(shape, dim):
    return lax.broadcasted_iota(I32, shape, dim)


def nt_dot(a, b):
    return lax.dot_general(a, b, (((1,), (1,)), ((), ())), preferred_element_type=F32)


def nn_dot(a, b):
    return jnp.dot(a, b, preferred_element_type=F32)


def segments(levels):
    segs = []
    low = 0
    for level in range(levels - 1, 1, -1):
        count = 2 ** (level - 1)
        segs.append((low, count))
        low += count
    segs.append((low, 2))
    return segs


def group_kernel(nx, ns, levels, cot_ref, pre_ref, mix_ref, lev_ref, pairs_ref, k1_hbm, k2_hbm,
                 grad_ref, wg_ref, rawx, raws, pre_s, pre_r, mix_s, mix_r, cot, pre,
                 mix, act, slope, work, refs, im, imw, imc, conv_out, out_r, rhs_buf, bands, kpad,
                 perm, comb, sel, back, part, ab_s, ab_r, rs_s, rs_r, ag_b, flat_f, whole, k1_ref, k2_ref,
                 lsem, ssem, rsem,
                 *halos):
    tm = lax.axis_index("tm")
    sp = lax.axis_index("space")
    xi = tm // 2
    core = tm % 2
    nt = 2 * nx
    fl, rows, width = cot_ref.shape
    frames = fl * nt
    half = frames // 2
    lanes = cot.shape[2]
    own = lanes - 1536
    span = own + 1024
    mid = slice(256, 256 + span)
    quads = lanes // 256
    inner_q = quads - 2
    wide = own // 256
    shard = part.shape[2]
    piece = ag_b.shape[3]
    hal_s, hal_r = halos[:levels], halos[levels:]
    down = (sp + 1) % ns
    up = (sp + ns - 1) % ns
    sib = (xi * 2 + 1 - core, sp)
    chip = rawx.shape[4] - 1024
    tms = [((tm + d) % nt, sp) for d in range(1, nt)]
    xs = [(((xi + d) % nx) * 2 + core, sp) for d in range(1, nx)]
    sps = [(tm, (sp + d) % ns) for d in range(1, ns)]

    barrier = pltpu.get_barrier_semaphore()
    for peer in tms + sps:
        pl.semaphore_signal(barrier, inc=1, device_id=peer, device_id_type=pl.DeviceIdType.MESH)
    slots = [0]

    def plan(src, dst, peer):
        copy = pltpu.make_async_remote_copy(
            src_ref=src, dst_ref=dst, send_sem=ssem.at[slots[0]], recv_sem=rsem.at[slots[0]],
            device_id=peer, device_id_type=pl.DeviceIdType.MESH)
        slots[0] += 1
        return copy

    def send(src, dst, peer):
        copy = plan(src, dst, peer)
        copy.start()
        return copy

    def exchange(held, landed):
        rise = plan(held.at[0], landed.at[1], (tm, up))
        fall = plan(held.at[1], landed.at[0], (tm, down))

        @pl.when(sp > 0)
        def _():
            rise.start()

        @pl.when(sp < ns - 1)
        def _():
            fall.start()

        return rise, fall

    def settle(pair):
        rise, fall = pair

        @pl.when(sp > 0)
        def _():
            rise.wait_send()
            fall.wait_recv()

        @pl.when(sp < ns - 1)
        def _():
            fall.wait_send()
            rise.wait_recv()

    sources = (cot_ref, pre_ref, mix_ref)
    targets = (cot, pre, mix)

    def chip_start(x):
        start = 2 * own * x - 512 * ((x + nx - 1) // nx)
        if nx > 2:
            start = start - 512 * (x // (nx - 1))
        return start

    def window(x, c):
        return pl.ds(pl.multiple_of((2 * x + c) * own - chip_start(x), 128), span)

    def send_chips(n):
        copies = []
        for d in range(1, nx):
            x = (xi + d) % nx
            cut = pl.ds(pl.multiple_of(chip_start(x), 128), chip)
            copies.append(send(sources[n].at[:, :, cut], rawx.at[n, xi, :, :, 512 : 512 + chip],
                               (x * 2 + core, sp)))
        return copies

    mine = pl.ds(pl.multiple_of(chip_start(xi), 128), chip)
    loads = [pltpu.make_async_copy(sources[n].at[:, :, mine],
                                   rawx.at[n, xi, :, :, 512 : 512 + chip], lsem.at[n])
             for n in range(3)]
    loads += [pltpu.make_async_copy(k1_hbm, k1_ref, lsem.at[3]),
              pltpu.make_async_copy(k2_hbm, k2_ref, lsem.at[4]),
              pltpu.make_async_copy(cot_ref, whole, lsem.at[5])]
    for n in (0, 1, 3, 4):
        loads[n].start()

    def pass_on(n, x):
        return send(rawx.at[n, x, :, :, window(xi, 1 - core)], raws.at[n, x], sib)

    pl.semaphore_wait(barrier, len(tms) + len(sps))
    across = [send_chips(0), send_chips(1)]
    rawx[:, :, :, :, 0:512] = jnp.zeros((3, nx, fl, rows, 512), BF)
    rawx[:, :, :, :, 512 + chip :] = jnp.zeros((3, nx, fl, rows, 512), BF)
    @pl.when(sp == 0)
    def _():
        for landed in (pre_r, mix_r) + tuple(hal_r):
            landed[0] = jnp.zeros(landed.shape[1:], BF)

    @pl.when(sp == ns - 1)
    def _():
        for landed in (pre_r, mix_r) + tuple(hal_r):
            landed[1] = jnp.zeros(landed.shape[1:], BF)

    passed = [[], [], []]
    for n in range(2):
        loads[n].wait()
        passed[n].append(pass_on(n, xi))
    loads[2].start()
    loads[5].start()
    for held in (cot, pre, mix, act):
        held[:, :, 0:256] = jnp.zeros((rows + 4, frames, 256), F32)
        held[:, :, lanes - 256 :] = jnp.zeros((rows + 4, frames, 256), F32)
    for r in (0, 1, rows + 2, rows + 3):
        cot[r] = jnp.zeros((frames, lanes), F32)
    work[...] = jnp.zeros_like(work)

    order_row = (levels - lev_ref[...]) * frames + iota((1, frames), 1)
    order_row = order_row.astype(F32)
    eye = iota((frames, frames), 0) == iota((frames, frames), 1)
    order_col = jnp.sum(jnp.where(eye, jnp.broadcast_to(order_row, (frames, frames)), 0.0),
                        axis=1, keepdims=True)
    rank_row = jnp.sum((order_col < order_row).astype(F32), axis=0, keepdims=True)
    hot = (iota((frames, frames), 0).astype(F32) == rank_row).astype(F32)
    total = frames * rows
    m_id = iota((total, frames), 0)
    to_slot = (mod(m_id, frames) == iota((total, frames), 1)).astype(F32)
    n_id = iota((frames, total), 1)
    side = div(n_id, rows * fl * nx)
    from_core = core + side - 2 * core * side
    from_frame = ((mod(div(n_id, rows * fl), nx) * 2 + from_core) * fl + mod(div(n_id, rows), fl))
    from_hot = (from_frame == iota((frames, total), 0)).astype(F32)
    same_row = div(iota((total, total), 0), frames) == mod(iota((total, total), 1), rows)
    perm[...] = jnp.where(same_row, nn_dot(to_slot, nn_dot(hot, from_hot)), 0.0).astype(BF)
    pairs = pairs_ref[...]
    ref_hot = 0.5 * ((pairs[0:1] == iota((frames, frames), 0)).astype(F32)
                     + (pairs[1:2] == iota((frames, frames), 0)).astype(F32))
    mixw = nt_dot(nn_dot(hot, ref_hot), hot)
    few = rows // 2 * half
    to_low = (mod(iota((few, frames), 0), half) + half == iota((few, frames), 1)).astype(F32)
    same_few = div(iota((few, few), 0), half) == div(iota((few, few), 1), half)
    for k in range(levels):
        g = 0 if k == levels - 1 else half
        lowest = frames - 2 ** (k + 1)
        s_id = mod(iota((frames, few), 1), half) + g
        on = jnp.logical_and(s_id >= lowest, s_id < lowest + 2**k)
        pick = jnp.logical_and(s_id == iota((frames, few), 0), on).astype(F32)
        comb[k] = jnp.where(same_few, nn_dot(nn_dot(to_low, mixw), pick), 0.0).astype(BF)
    low_rows = rows * half
    local = (div(iota((fl * rows, frames), 0), rows) + tm * fl
             == iota((fl * rows, frames), 1)).astype(F32)
    local_hot = nt_dot(local, hot)
    top = jnp.sum(jnp.where(iota((fl * rows, frames), 1) < half, local_hot, 0.0),
                  axis=1, keepdims=True)
    segs = segments(levels)
    o_id = iota((frames, low_rows), 1)
    o_row = mod(iota((fl * rows, low_rows), 0), rows)
    p_id = iota((fl * rows, low_rows), 1)
    slot_of = jnp.zeros_like(o_id)
    row_of = jnp.zeros_like(p_id)
    for low, count in segs:
        here = o_id >= low * rows
        slot_of = jnp.where(here, half + low + mod(o_id - low * rows, count), slot_of)
        there = p_id >= low * rows
        row_of = jnp.where(there, div(p_id - low * rows, count), row_of)
    back[...] = jnp.where(o_row == row_of, nn_dot(
        local_hot, (slot_of == iota((frames, low_rows), 0)).astype(F32)), 0.0).astype(BF)
    for low, count in segs:
        size = rows * count
        a_id = iota((size, low_rows), 0)
        b_id = iota((size, low_rows), 1)
        sel[low * rows : low * rows + size] = jnp.logical_and(
            div(a_id, count) == div(b_id, half),
            low + mod(a_id, count) == mod(b_id, half)).astype(F32).astype(BF)

    bands[...] = jnp.zeros_like(bands)
    loads[3].wait()
    loads[4].wait()
    kpad[0:64] = jnp.zeros((64, 64), BF)
    kpad[256:320] = jnp.zeros((64, 64), BF)
    unit = (iota((64, 64), 0) == iota((64, 64), 1)).astype(F32).astype(BF)
    for n in range(2):
        for k in range(levels):
            for a in range(3):
                kpad[64:256] = (k2_ref, k1_ref)[n][k, 2 - a]
                even = nt_dot(unit, kpad[64:320]).astype(BF)
                odd = nt_dot(unit, kpad[0:256]).astype(BF)
                bands[n, k, a, 64:128, 0:128] = even[:, 128:256]
                bands[n, k, a, 128:192, 0:128] = odd[:, 128:256]
                bands[n, k, a, 192:256] = even
                bands[n, k, a, 256:320] = odd
                bands[n, k, a, 320:384, 128:256] = even[:, 0:128]
                bands[n, k, a, 384:448, 128:256] = odd[:, 0:128]

    def gather(n):
        for i, copy in enumerate(across[n]):
            copy.wait()
            passed[n].append(pass_on(n, (xi + nx - 1 - i) % nx))
        for copy in passed[n]:
            copy.wait()
        mine = (2 * xi + core) * own - chip_start(xi)
        for j in range(inner_q):
            cut = pl.ds(pl.multiple_of(mine + 256 * j, 128), 256)
            one = rawx[n, :, :, :, cut].astype(F32).reshape(total // 2, 256)
            two = raws[n, :, :, :, 256 * j : 256 * j + 256].astype(F32).reshape(total // 2, 256)
            block = jnp.concatenate((one, two), axis=0).astype(BF)
            moved = nn_dot(perm[...], block)
            targets[n][2 : 2 + rows, :, 256 * j + 256 : 256 * j + 512] = moved.reshape(
                rows, frames, 256)

    def reach(k):
        low = frames - 2 ** (k + 1)
        return slice(low, low + 2**k), slice(768 - 128 * (k + 1), 768 + own + 128 * (k + 1))

    def push(k):
        held, cut = reach(k)
        shape = hal_s[k].shape[1:]
        hal_s[k][0] = cot[2:4, held, cut].reshape(shape).astype(BF)
        hal_s[k][1] = cot[rows : rows + 2, held, cut].reshape(shape).astype(BF)
        return exchange(hal_s[k], hal_r[k])

    def land(k, flight):
        settle(flight)
        held, cut = reach(k)
        shape = (2, 2**k, hal_s[k].shape[2])
        cot[0:2, held, cut] = hal_r[k][0].astype(F32).reshape(shape) * has_up
        cot[rows + 2 : rows + 4, held, cut] = hal_r[k][1].astype(F32).reshape(shape) * has_down

    has_up = (sp > 0).astype(F32)
    has_down = (sp < ns - 1).astype(F32)
    column = iota((8, lanes), 1) + tm * own - 768
    inside = jnp.logical_and(column >= 0, column < own * nt).astype(F32)

    gather(0)
    flight = push(levels - 1)
    gather(1)
    across.append(send_chips(2))
    loads[2].wait()
    passed[2].append(pass_on(2, xi))
    pre_s[0] = pre[2, :, mid].astype(BF)
    pre_s[1] = pre[rows + 1, :, mid].astype(BF)
    edges = exchange(pre_s, pre_r)

    def activate(r):
        gate = has_up if r == 0 else (has_down if r == rows + 1 else 1.0)
        for g in range(0, frames, 8):
            v = pre[r + 1, g : g + 8, mid]
            sig = jax.nn.sigmoid(v)
            slope[r, g : g + 8, mid] = sig * (1.0 + v * (1.0 - sig)) * inside[:, mid] * gate
            act[r + 1, g : g + 8, mid] = v * sig

    def fill(dest, source, g, first, spans, base, width):
        for low, count in spans:
            for r in range(low, low + count):
                for j in range(0, width, 2):
                    lo = 256 * (base + j) - 128
                    one = source[first + r, g : g + 8, lo : lo + 512]
                    two = source[first + r, g : g + 8, lo + 256 : lo + 768]
                    dest[r, 8 * j : 8 * j + 16] = jnp.concatenate((one, two), axis=0).astype(BF)

    def conv(source, n, k, spans, base, width, store):
        total = None
        for a in range(3):
            lhs = [source[low + a : low + a + count, 0 : 8 * width].reshape(count * 8 * width, 512)
                   for low, count in spans]
            lhs = lhs[0] if len(lhs) == 1 else jnp.concatenate(lhs, axis=0)
            term = nn_dot(lhs, bands[n, k, a])
            total = term if total is None else total + term
        conv_out[0 : total.shape[0]] = total
        at = 0
        for low, count in spans:
            for r in range(low, low + count):
                for j in range(width):
                    store(r, base + j, conv_out[at : at + 8])
                    at += 8

    slot_no = iota((8, 256), 0) + 8

    tall = 8 * wide

    def keep_pair(k):
        g = 0 if k == levels - 1 else half
        lowest = frames - 2 ** (k + 1)
        active = jnp.logical_and(slot_no >= lowest, slot_no < lowest + 2**k)
        for n in range(2):
            for r in range(rows):
                for j in range(0, wide, 2):
                    cut = 768 + 256 * j
                    if n == 0:
                        left = work[1 + r, :, cut : cut + 256]
                        right = work[1 + r, :, cut + 256 : cut + 512]
                    else:
                        left = cot[2 + r, g : g + 8, cut : cut + 256]
                        right = cot[2 + r, g : g + 8, cut + 256 : cut + 512]
                    if g:
                        left = jnp.where(active, left, 0.0)
                        right = jnp.where(active, right, 0.0)
                    rhs_buf[k, n, r, 8 * j : 8 * j + 16] = jnp.concatenate(
                        (left, right), axis=0).astype(BF)

    def correlate(k):
        step = math.gcd(192, shard)
        for a in range(3):
            both = []
            for n in range(2):
                rhs = rhs_buf[k, n].reshape(rows * tall, 256)
                lhs = imc[n, 0 if k == levels - 1 else 1, a : a + rows].reshape(rows * tall, 512)
                block = lax.dot_general(
                    lhs, rhs, (((0,), (0,)), ((), ())), preferred_element_type=F32)
                taps = block[64:256, 0:64]
                for p in range(1, 4):
                    taps = taps + block[64 * (p + 1) : 64 * (p + 4), 64 * p : 64 * p + 64]
                both.append(taps)
            joint = jnp.concatenate(both, axis=1) * (1.0 / math.sqrt(rows * ns * (own * nt // 64)))
            for i in range(0, 192, step):
                at = 192 * a + i
                part[k, at // shard, at % shard : at % shard + step] = joint[i : i + step]
        for t in range(nt):
            ab_s[k, t] = part[k, t].astype(BF)
        stage[k] = [send(ab_s.at[k, peer[0]], ab_r.at[k, tm], peer) for peer in tms]

    def arrive(k):
        for copy in stage[k]:
            copy.wait()

    def scatter(k):
        arrive(k)
        value = part[k, tm]
        for d in range(1, nt):
            value = value + ab_r[k, (tm + d) % nt].astype(F32)
        flat_f[0:shard] = value
        for i in range(ns):
            rs_s[k, i] = flat_f[piece * i : piece * i + piece].astype(BF)
        stage[k] = [send(rs_s.at[k, peer[1]], rs_r.at[k, sp], peer) for peer in sps]

    def spread(k):
        arrive(k)
        value = rs_s[k, sp].astype(F32)
        for d in range(1, ns):
            value = value + rs_r[k, (sp + d) % ns].astype(F32)
        ag_b[k, tm, sp] = value.astype(BF)
        stage[k] = [send(ag_b.at[k, tm, sp], ag_b.at[k, tm, sp], peer) for peer in sps]

    def share(k):
        arrive(k)
        stage[k] = [send(ag_b.at[k, tm], ag_b.at[k, tm], peer) for peer in tms]

    def finish(k):
        arrive(k)
        for t in range(nt):
            for i in range(ns):
                flat_f[piece * i : piece * i + piece] = ag_b[k, t, i].astype(F32)
            wg_ref[k, t] = flat_f[0:shard].astype(BF)

    def hand_out(low, count):
        a, b = low * rows, (low + count) * rows
        for j in range(wide):
            cut = slice(768 + 256 * j, 1024 + 256 * j)
            flat = cot[2 : 2 + rows, half:, cut].reshape(low_rows, 256).astype(BF)
            out_r[tm, a:b, 256 * j : 256 * j + 256] = nn_dot(sel[a:b], flat).astype(BF)
        return [send(out_r.at[tm, a:b], out_r.at[tm, a:b], peer) for peer in xs + [sib]]

    def hand_on(low, count, copies):
        a, b = low * rows, (low + count) * rows
        later = copies[-1:]
        for i, copy in enumerate(copies[:-1]):
            copy.wait()
            source = ((xi + nx - 1 - i) % nx) * 2 + core
            later.append(send(out_r.at[source, a:b], out_r.at[source, a:b], sib))
        return later

    stage = {}
    quarter = rows // 4
    inner_one = [(2, rows - 2)]
    outer_one = [(0, 2), (rows, 2)]
    inner_two = [(quarter, rows - 2 * quarter)]
    outer_two = [(0, quarter), (rows - quarter, quarter)]

    def tile(k):
        return 0 if k == levels - 1 else half

    def put_grad(k):
        g = tile(k)

        def store(r, j, block):
            cut = slice(256 * j, 256 * j + 256)
            work[r, :, cut] = (block * slope[r, g : g + 8, cut]).astype(BF).astype(F32)

        return store

    def put_refs(r, j, block):
        cut = slice(256 * j, 256 * j + 256)
        refs[r, :, cut] = block * inside[:, cut]

    def combine(k, spans, base, width):
        for j in range(base, base + width):
            cut = slice(256 * j, 256 * j + 256)
            block = jnp.concatenate([refs[low : low + count, :, cut].reshape(count * 8, 256)
                                     for low, count in spans], axis=0).astype(BF)
            extra = nn_dot(comb[k], block)
            at = 0
            for low, count in spans:
                cot[2 + low : 2 + low + count, half:, cut] += extra[
                    at : at + count * half].reshape(count, half, 256)
                at += count * half

    def bounds(k, n):
        skip = 2 - -(-(2 * k + 1 - n) // 4)
        return 1 + skip, inner_q - 2 * skip

    def first(k, cells, landed):
        base, width = bounds(k, 0)
        fill(im, cot, tile(k), 0, landed, base, width)
        conv(im, 0, k, cells, base, width, put_grad(k))

    def second(k, cells, landed):
        base, width = bounds(k, 1)
        fill(imw, work, 0, 0, landed, base, width)
        conv(imw, 1, k, cells, base, width, put_refs)
        combine(k, cells, base, width)

    top_level = levels - 1
    for r in range(1, rows + 1):
        activate(r)
    first(top_level, inner_one, [(2, rows)])
    settle(edges)
    pre[1, :, mid] = pre_r[0].astype(F32) * has_up
    pre[rows + 2, :, mid] = pre_r[1].astype(F32) * has_down
    activate(0)
    activate(rows + 1)
    moving = []
    for k in range(top_level, -1, -1):
        land(k, flight)
        first(k, outer_one, [(0, 2), (rows + 2, 2)])
        if k == 0:
            keep_pair(0)
            correlate(0)
            scatter(1)
        second(k, outer_two, [(0, rows + 2)])
        if k > 0:
            flight = push(k - 1)
        if k == 1:
            scatter(3)
            scatter(2)
        second(k, inner_two, [])
        if k > 0:
            keep_pair(k)
            first(k - 1, inner_one, [(2, rows)])
        if k == 3:
            fill(imc.at[1, 0], act, 0, 1, [(0, rows + 2)], 3, wide)
            fill(imc.at[1, 1], act, half, 1, [(0, rows + 2)], 3, wide)
            moving.append((segs[0], hand_out(*segs[0])))
            gather(2)
            trim = slice(640, 896 + own)
            mix_s[0] = mix[2, :, trim].astype(BF)
            mix_s[1] = mix[rows + 1, :, trim].astype(BF)
            edges = exchange(mix_s, mix_r)
        if k == 2:
            moving.append((segs[1], hand_out(*segs[1])))
            moving[0] = (segs[0], hand_on(*moving[0][0], moving[0][1]))
            settle(edges)
            mix[1, :, trim] = mix_r[0].astype(F32) * has_up
            mix[rows + 2, :, trim] = mix_r[1].astype(F32) * has_down
            fill(imc.at[0, 0], mix, 0, 1, [(0, rows + 2)], 3, wide)
            fill(imc.at[0, 1], mix, half, 1, [(0, rows + 2)], 3, wide)
            correlate(3)
            correlate(2)
        if k == 1:
            moving[1] = (segs[1], hand_on(*moving[1][0], moving[1][1]))
            correlate(1)
            spread(3)
            spread(2)
    moving.append((segs[2], hand_out(*segs[2])))
    scatter(0)
    spread(1)
    share(3)
    share(2)
    moving[2] = (segs[2], hand_on(*moving[2][0], moving[2][1]))
    spread(0)
    share(1)
    loads[5].wait()
    finish(3)
    finish(2)
    for _, copies in moving:
        for copy in copies:
            copy.wait()
    for t in range(nt):
        for j in range(wide):
            cut = slice(own * t + 256 * j, own * t + 256 * j + 256)
            plain = whole[:, :, cut].astype(F32).reshape(fl * rows, 256)
            value = nn_dot(back[...], out_r[t, :, 256 * j : 256 * j + 256]) + top * plain
            grad_ref[:, cut] = value.astype(BF)
    share(0)
    finish(1)
    finish(0)


def widen_kernel(grad_ref, wg_ref, out_ref, one_ref, two_ref):
    out_ref[...] = grad_ref[...].astype(F32)
    one_ref[...] = wg_ref[:, 0:64].astype(F32)
    two_ref[...] = wg_ref[:, 64:128].astype(F32)


def on_device(cotangent, saved_mix, saved_pre, kernel_one, kernel_two, ref_pairs, frame_level):
    fl, rows, width = cotangent.shape
    nt = lax.axis_size("tm")
    nx = nt // 2
    ns = lax.axis_size("space")
    levels = kernel_one.shape[0]
    frames = fl * nt
    half = frames // 2
    own = width // nt
    lanes = own + 1536
    span = own + 1024
    quads = lanes // 256
    wide = own // 256
    chip = 2 * own + (512 if nx <= 2 else 1024)
    shard = 576 // nt
    tall = rows + 4
    few = rows // 2 * half
    vmem = pl.BlockSpec(memory_space=pltpu.VMEM)
    hbm = pl.BlockSpec(memory_space=pl.ANY)
    piece = -(-shard // ns)
    count = (3 * (nx - 1) + 3 * nx + 4 + 2 * levels + (levels - 1) * (2 * nx - 1)
             + 2 * levels * (nt - 1 + ns - 1))
    halo = [pltpu.VMEM((2, 2 * 2**k, own + 256 * (k + 1)), BF) for k in range(levels)]
    grad, wg = pl.pallas_call(
        functools.partial(group_kernel, nx, ns, levels),
        out_shape=(
            jax.ShapeDtypeStruct((fl * rows, width), BF),
            jax.ShapeDtypeStruct((levels, nt, shard, 128), BF),
        ),
        in_specs=[hbm] * 3 + [vmem] * 2 + [hbm] * 2,
        out_specs=(vmem, vmem),
        scratch_shapes=[
            pltpu.VMEM((3, nx, fl, rows, chip + 1024), BF),
            pltpu.VMEM((3, nx, fl, rows, span), BF),
            pltpu.VMEM((2, frames, span), BF),
            pltpu.VMEM((2, frames, span), BF),
            pltpu.VMEM((2, frames, own + 256), BF),
            pltpu.VMEM((2, frames, own + 256), BF),
            pltpu.VMEM((tall, frames, lanes), F32),
            pltpu.VMEM((tall, frames, lanes), F32),
            pltpu.VMEM((tall, frames, lanes), F32),
            pltpu.VMEM((tall, frames, lanes), F32),
            pltpu.VMEM((rows + 2, frames, lanes), F32),
            pltpu.VMEM((rows + 2, 8, lanes), F32),
            pltpu.VMEM((rows, 8, lanes), F32),
            pltpu.VMEM((tall, 8 * (quads - 2), 512), BF),
            pltpu.VMEM((rows + 2, 8 * (quads - 2), 512), BF),
            pltpu.VMEM((2, 2, rows + 2, 8 * wide, 512), BF),
            pltpu.VMEM(((rows - 2) * 8 * (quads - 2), 256), F32),
            pltpu.VMEM((nt, rows * half, own), BF),
            pltpu.VMEM((levels, 2, rows, 8 * wide, 256), BF),
            pltpu.VMEM((2, levels, 3, 512, 256), BF),
            pltpu.VMEM((320, 64), BF),
            pltpu.VMEM((rows * frames, rows * frames), BF),
            pltpu.VMEM((levels, few, few), BF),
            pltpu.VMEM((rows * half, rows * half), BF),
            pltpu.VMEM((fl * rows, rows * half), BF),
            pltpu.VMEM((levels, nt, shard, 128), F32),
            pltpu.VMEM((levels, nt, shard, 128), BF),
            pltpu.VMEM((levels, nt, shard, 128), BF),
            pltpu.VMEM((levels, ns, piece, 128), BF),
            pltpu.VMEM((levels, ns, piece, 128), BF),
            pltpu.VMEM((levels, nt, ns, piece, 128), BF),
            pltpu.VMEM((ns * piece, 128), F32),
            pltpu.VMEM((fl, rows, width), BF),
            pltpu.VMEM((levels, 3, 192, 64), BF),
            pltpu.VMEM((levels, 3, 192, 64), BF),
            pltpu.SemaphoreType.DMA((6,)),
            pltpu.SemaphoreType.DMA((count,)),
            pltpu.SemaphoreType.DMA((count,)),
        ] + halo + halo,
        compiler_params=pltpu.CompilerParams(
            collective_id=3, has_side_effects=True, vmem_limit_bytes=60 * 2**20
        ),
        name="group",
    )(cotangent, saved_pre, saved_mix, frame_level.reshape(1, frames), ref_pairs.T,
      kernel_one.reshape(levels, 3, 192, 64), kernel_two.reshape(levels, 3, 192, 64))
    grad, one, two = pl.pallas_call(
        widen_kernel,
        grid=(levels,),
        out_shape=(
            jax.ShapeDtypeStruct((fl * rows, width), F32),
            jax.ShapeDtypeStruct((levels * 576, 64), F32),
            jax.ShapeDtypeStruct((levels * 576, 64), F32),
        ),
        in_specs=[pl.BlockSpec((fl * rows, width // levels), lambda i: (0, i)),
                  pl.BlockSpec((576, 128), lambda i: (i, 0))],
        out_specs=(pl.BlockSpec((fl * rows, width // levels), lambda i: (0, i)),
                   pl.BlockSpec((576, 64), lambda i: (i, 0)),
                   pl.BlockSpec((576, 64), lambda i: (i, 0))),
        name="widen",
    )(grad, wg.reshape(levels * 576, 128))
    return (grad.reshape(cotangent.shape), one.reshape(kernel_one.shape),
            two.reshape(kernel_one.shape))


def solution(mesh):
    placed = (
        P("tm", "space", None),
        P("tm", "space", None),
        P("tm", "space", None),
        P(),
        P(),
        P(),
        P(),
    )
    return jax.shard_map(
        on_device,
        mesh=mesh,
        in_specs=placed,
        out_specs=(P("tm", "space", None), P(), P()),
        check_vma=False,
    )
```

```python
import functools
import math

import jax
import jax.numpy as jnp
from jax import lax
from jax.experimental import pallas as pl
from jax.experimental.pallas import tpu as pltpu
from jax.sharding import PartitionSpec as P

BF = jnp.bfloat16
F32 = jnp.float32
I32 = jnp.int32


def div(value, n):
    return lax.shift_right_logical(value, jnp.full_like(value, n.bit_length() - 1))


def mod(value, n):
    return jnp.bitwise_and(value, n - 1)


def iota(shape, dim):
    return lax.broadcasted_iota(I32, shape, dim)


def nt_dot(a, b):
    return lax.dot_general(a, b, (((1,), (1,)), ((), ())), preferred_element_type=F32)


def nn_dot(a, b):
    return jnp.dot(a, b, preferred_element_type=F32)


def segments(levels):
    segs = []
    low = 0
    for level in range(levels - 1, 1, -1):
        count = 2 ** (level - 1)
        segs.append((low, count))
        low += count
    segs.append((low, 2))
    return segs


def group_kernel(nx, ns, levels, cot_ref, pre_ref, mix_ref, lev_ref, pairs_ref, k1_hbm, k2_hbm,
                 grad_ref, wg_ref, rawx, raws, pre_s, pre_r, mix_s, mix_r, cot, pre,
                 mix, act, slope, work, refs, im, imw, imc, conv_out, out_r, rhs_buf, bands, kpad,
                 perm, comb, sel, back, part, ab_s, ab_r, rs_s, rs_r, ag_b, flat_f, whole, k1_ref, k2_ref,
                 lsem, ssem, rsem,
                 *halos):
    tm = lax.axis_index("tm")
    sp = lax.axis_index("space")
    xi = tm // 2
    core = tm % 2
    nt = 2 * nx
    fl, rows, width = cot_ref.shape
    frames = fl * nt
    half = frames // 2
    lanes = cot.shape[2]
    own = lanes - 1536
    span = own + 1024
    mid = slice(256, 256 + span)
    quads = lanes // 256
    inner_q = quads - 2
    wide = own // 256
    shard = part.shape[2]
    piece = ag_b.shape[3]
    hal_s, hal_r = halos[:levels], halos[levels:]
    down = (sp + 1) % ns
    up = (sp + ns - 1) % ns
    sib = (xi * 2 + 1 - core, sp)
    chip = rawx.shape[4] - 1024
    tms = [((tm + d) % nt, sp) for d in range(1, nt)]
    xs = [(((xi + d) % nx) * 2 + core, sp) for d in range(1, nx)]
    sps = [(tm, (sp + d) % ns) for d in range(1, ns)]

    barrier = pltpu.get_barrier_semaphore()
    for peer in tms + sps:
        pl.semaphore_signal(barrier, inc=1, device_id=peer, device_id_type=pl.DeviceIdType.MESH)
    slots = [0]

    def plan(src, dst, peer):
        copy = pltpu.make_async_remote_copy(
            src_ref=src, dst_ref=dst, send_sem=ssem.at[slots[0]], recv_sem=rsem.at[slots[0]],
            device_id=peer, device_id_type=pl.DeviceIdType.MESH)
        slots[0] += 1
        return copy

    def send(src, dst, peer):
        copy = plan(src, dst, peer)
        copy.start()
        return copy

    def exchange(held, landed):
        rise = plan(held.at[0], landed.at[1], (tm, up))
        fall = plan(held.at[1], landed.at[0], (tm, down))

        @pl.when(sp > 0)
        def _():
            rise.start()

        @pl.when(sp < ns - 1)
        def _():
            fall.start()

        return rise, fall

    def settle(pair):
        rise, fall = pair

        @pl.when(sp > 0)
        def _():
            rise.wait_send()
            fall.wait_recv()

        @pl.when(sp < ns - 1)
        def _():
            fall.wait_send()
            rise.wait_recv()

    sources = (cot_ref, pre_ref, mix_ref)
    targets = (cot, pre, mix)

    def chip_start(x):
        start = 2 * own * x - 512 * ((x + nx - 1) // nx)
        if nx > 2:
            start = start - 512 * (x // (nx - 1))
        return start

    def window(x, c):
        return pl.ds(pl.multiple_of((2 * x + c) * own - chip_start(x), 128), span)

    def send_chips(n):
        copies = []
        for d in range(1, nx):
            x = (xi + d) % nx
            cut = pl.ds(pl.multiple_of(chip_start(x), 128), chip)
            copies.append(send(sources[n].at[:, :, cut], rawx.at[n, xi, :, :, 512 : 512 + chip],
                               (x * 2 + core, sp)))
        return copies

    mine = pl.ds(pl.multiple_of(chip_start(xi), 128), chip)
    loads = [pltpu.make_async_copy(sources[n].at[:, :, mine],
                                   rawx.at[n, xi, :, :, 512 : 512 + chip], lsem.at[n])
             for n in range(3)]
    loads += [pltpu.make_async_copy(k1_hbm, k1_ref, lsem.at[3]),
              pltpu.make_async_copy(k2_hbm, k2_ref, lsem.at[4]),
              pltpu.make_async_copy(cot_ref, whole, lsem.at[5])]
    for n in (0, 1, 3, 4):
        loads[n].start()

    def pass_on(n, x):
        return send(rawx.at[n, x, :, :, window(xi, 1 - core)], raws.at[n, x], sib)

    pl.semaphore_wait(barrier, len(tms) + len(sps))
    across = [send_chips(0), send_chips(1)]
    rawx[:, :, :, :, 0:512] = jnp.zeros((3, nx, fl, rows, 512), BF)
    rawx[:, :, :, :, 512 + chip :] = jnp.zeros((3, nx, fl, rows, 512), BF)
    @pl.when(sp == 0)
    def _():
        for landed in (pre_r, mix_r) + tuple(hal_r):
            landed[0] = jnp.zeros(landed.shape[1:], BF)

    @pl.when(sp == ns - 1)
    def _():
        for landed in (pre_r, mix_r) + tuple(hal_r):
            landed[1] = jnp.zeros(landed.shape[1:], BF)

    passed = [[], [], []]
    for n in range(2):
        loads[n].wait()
        passed[n].append(pass_on(n, xi))
    loads[2].start()
    loads[5].start()
    for held in (cot, pre, mix, act):
        held[:, :, 0:256] = jnp.zeros((rows + 4, frames, 256), F32)
        held[:, :, lanes - 256 :] = jnp.zeros((rows + 4, frames, 256), F32)
    for r in (0, 1, rows + 2, rows + 3):
        cot[r] = jnp.zeros((frames, lanes), F32)
    work[...] = jnp.zeros_like(work)

    order_row = (levels - lev_ref[...]) * frames + iota((1, frames), 1)
    order_row = order_row.astype(F32)
    eye = iota((frames, frames), 0) == iota((frames, frames), 1)
    order_col = jnp.sum(jnp.where(eye, jnp.broadcast_to(order_row, (frames, frames)), 0.0),
                        axis=1, keepdims=True)
    rank_row = jnp.sum((order_col < order_row).astype(F32), axis=0, keepdims=True)
    hot = (iota((frames, frames), 0).astype(F32) == rank_row).astype(F32)
    total = frames * rows
    m_id = iota((total, frames), 0)
    to_slot = (mod(m_id, frames) == iota((total, frames), 1)).astype(F32)
    n_id = iota((frames, total), 1)
    side = div(n_id, rows * fl * nx)
    from_core = core + side - 2 * core * side
    from_frame = ((mod(div(n_id, rows * fl), nx) * 2 + from_core) * fl + mod(div(n_id, rows), fl))
    from_hot = (from_frame == iota((frames, total), 0)).astype(F32)
    same_row = div(iota((total, total), 0), frames) == mod(iota((total, total), 1), rows)
    perm[...] = jnp.where(same_row, nn_dot(to_slot, nn_dot(hot, from_hot)), 0.0).astype(BF)
    pairs = pairs_ref[...]
    ref_hot = 0.5 * ((pairs[0:1] == iota((frames, frames), 0)).astype(F32)
                     + (pairs[1:2] == iota((frames, frames), 0)).astype(F32))
    mixw = nt_dot(nn_dot(hot, ref_hot), hot)
    few = rows // 2 * half
    to_low = (mod(iota((few, frames), 0), half) + half == iota((few, frames), 1)).astype(F32)
    same_few = div(iota((few, few), 0), half) == div(iota((few, few), 1), half)
    for k in range(levels):
        g = 0 if k == levels - 1 else half
        lowest = frames - 2 ** (k + 1)
        s_id = mod(iota((frames, few), 1), half) + g
        on = jnp.logical_and(s_id >= lowest, s_id < lowest + 2**k)
        pick = jnp.logical_and(s_id == iota((frames, few), 0), on).astype(F32)
        comb[k] = jnp.where(same_few, nn_dot(nn_dot(to_low, mixw), pick), 0.0).astype(BF)
    low_rows = rows * half
    local = (div(iota((fl * rows, frames), 0), rows) + tm * fl
             == iota((fl * rows, frames), 1)).astype(F32)
    local_hot = nt_dot(local, hot)
    top = jnp.sum(jnp.where(iota((fl * rows, frames), 1) < half, local_hot, 0.0),
                  axis=1, keepdims=True)
    segs = segments(levels)
    o_id = iota((frames, low_rows), 1)
    o_row = mod(iota((fl * rows, low_rows), 0), rows)
    p_id = iota((fl * rows, low_rows), 1)
    slot_of = jnp.zeros_like(o_id)
    row_of = jnp.zeros_like(p_id)
    for low, count in segs:
        here = o_id >= low * rows
        slot_of = jnp.where(here, half + low + mod(o_id - low * rows, count), slot_of)
        there = p_id >= low * rows
        row_of = jnp.where(there, div(p_id - low * rows, count), row_of)
    back[...] = jnp.where(o_row == row_of, nn_dot(
        local_hot, (slot_of == iota((frames, low_rows), 0)).astype(F32)), 0.0).astype(BF)
    for low, count in segs:
        size = rows * count
        a_id = iota((size, low_rows), 0)
        b_id = iota((size, low_rows), 1)
        sel[low * rows : low * rows + size] = jnp.logical_and(
            div(a_id, count) == div(b_id, half),
            low + mod(a_id, count) == mod(b_id, half)).astype(F32).astype(BF)

    bands[...] = jnp.zeros_like(bands)
    loads[3].wait()
    loads[4].wait()
    kpad[0:64] = jnp.zeros((64, 64), BF)
    kpad[256:320] = jnp.zeros((64, 64), BF)
    unit = (iota((64, 64), 0) == iota((64, 64), 1)).astype(F32).astype(BF)
    for n in range(2):
        for k in range(levels):
            for a in range(3):
                kpad[64:256] = (k2_ref, k1_ref)[n][k, 2 - a]
                even = nt_dot(unit, kpad[64:320]).astype(BF)
                odd = nt_dot(unit, kpad[0:256]).astype(BF)
                bands[n, k, a, 64:128, 0:128] = even[:, 128:256]
                bands[n, k, a, 128:192, 0:128] = odd[:, 128:256]
                bands[n, k, a, 192:256] = even
                bands[n, k, a, 256:320] = odd
                bands[n, k, a, 320:384, 128:256] = even[:, 0:128]
                bands[n, k, a, 384:448, 128:256] = odd[:, 0:128]

    def gather(n):
        for i, copy in enumerate(across[n]):
            copy.wait()
            passed[n].append(pass_on(n, (xi + nx - 1 - i) % nx))
        for copy in passed[n]:
            copy.wait()
        mine = (2 * xi + core) * own - chip_start(xi)
        for j in range(inner_q):
            cut = pl.ds(pl.multiple_of(mine + 256 * j, 128), 256)
            one = rawx[n, :, :, :, cut].astype(F32).reshape(total // 2, 256)
            two = raws[n, :, :, :, 256 * j : 256 * j + 256].astype(F32).reshape(total // 2, 256)
            block = jnp.concatenate((one, two), axis=0).astype(BF)
            moved = nn_dot(perm[...], block)
            targets[n][2 : 2 + rows, :, 256 * j + 256 : 256 * j + 512] = moved.reshape(
                rows, frames, 256)

    def reach(k):
        low = frames - 2 ** (k + 1)
        return slice(low, low + 2**k), slice(768 - 128 * (k + 1), 768 + own + 128 * (k + 1))

    def push(k):
        held, cut = reach(k)
        shape = hal_s[k].shape[1:]
        hal_s[k][0] = cot[2:4, held, cut].reshape(shape).astype(BF)
        hal_s[k][1] = cot[rows : rows + 2, held, cut].reshape(shape).astype(BF)
        return exchange(hal_s[k], hal_r[k])

    def land(k, flight):
        settle(flight)
        held, cut = reach(k)
        shape = (2, 2**k, hal_s[k].shape[2])
        cot[0:2, held, cut] = hal_r[k][0].astype(F32).reshape(shape) * has_up
        cot[rows + 2 : rows + 4, held, cut] = hal_r[k][1].astype(F32).reshape(shape) * has_down

    has_up = (sp > 0).astype(F32)
    has_down = (sp < ns - 1).astype(F32)
    column = iota((8, lanes), 1) + tm * own - 768
    inside = jnp.logical_and(column >= 0, column < own * nt).astype(F32)

    gather(0)
    flight = push(levels - 1)
    gather(1)
    across.append(send_chips(2))
    loads[2].wait()
    passed[2].append(pass_on(2, xi))
    pre_s[0] = pre[2, :, mid].astype(BF)
    pre_s[1] = pre[rows + 1, :, mid].astype(BF)
    edges = exchange(pre_s, pre_r)

    def activate(r):
        gate = has_up if r == 0 else (has_down if r == rows + 1 else 1.0)
        for g in range(0, frames, 8):
            v = pre[r + 1, g : g + 8, mid]
            sig = jax.nn.sigmoid(v)
            slope[r, g : g + 8, mid] = sig * (1.0 + v * (1.0 - sig)) * inside[:, mid] * gate
            act[r + 1, g : g + 8, mid] = v * sig

    def fill(dest, source, g, first, spans, base, width):
        for low, count in spans:
            for r in range(low, low + count):
                for j in range(0, width, 2):
                    lo = 256 * (base + j) - 128
                    one = source[first + r, g : g + 8, lo : lo + 512]
                    two = source[first + r, g : g + 8, lo + 256 : lo + 768]
                    dest[r, 8 * j : 8 * j + 16] = jnp.concatenate((one, two), axis=0).astype(BF)

    def conv(source, n, k, spans, base, width, store):
        total = None
        for a in range(3):
            lhs = [source[low + a : low + a + count, 0 : 8 * width].reshape(count * 8 * width, 512)
                   for low, count in spans]
            lhs = lhs[0] if len(lhs) == 1 else jnp.concatenate(lhs, axis=0)
            term = nn_dot(lhs, bands[n, k, a])
            total = term if total is None else total + term
        conv_out[0 : total.shape[0]] = total
        at = 0
        for low, count in spans:
            for r in range(low, low + count):
                for j in range(width):
                    store(r, base + j, conv_out[at : at + 8])
                    at += 8

    slot_no = iota((8, 256), 0) + 8

    tall = 8 * wide

    def keep_pair(k):
        g = 0 if k == levels - 1 else half
        lowest = frames - 2 ** (k + 1)
        active = jnp.logical_and(slot_no >= lowest, slot_no < lowest + 2**k)
        for n in range(2):
            for r in range(rows):
                for j in range(0, wide, 2):
                    cut = 768 + 256 * j
                    if n == 0:
                        left = work[1 + r, :, cut : cut + 256]
                        right = work[1 + r, :, cut + 256 : cut + 512]
                    else:
                        left = cot[2 + r, g : g + 8, cut : cut + 256]
                        right = cot[2 + r, g : g + 8, cut + 256 : cut + 512]
                    if g:
                        left = jnp.where(active, left, 0.0)
                        right = jnp.where(active, right, 0.0)
                    rhs_buf[k, n, r, 8 * j : 8 * j + 16] = jnp.concatenate(
                        (left, right), axis=0).astype(BF)

    def correlate(k):
        step = math.gcd(192, shard)
        for a in range(3):
            both = []
            for n in range(2):
                rhs = rhs_buf[k, n].reshape(rows * tall, 256)
                lhs = imc[n, 0 if k == levels - 1 else 1, a : a + rows].reshape(rows * tall, 512)
                block = lax.dot_general(
                    lhs, rhs, (((0,), (0,)), ((), ())), preferred_element_type=F32)
                taps = block[64:256, 0:64]
                for p in range(1, 4):
                    taps = taps + block[64 * (p + 1) : 64 * (p + 4), 64 * p : 64 * p + 64]
                both.append(taps)
            joint = jnp.concatenate(both, axis=1) * (1.0 / math.sqrt(rows * ns * (own * nt // 64)))
            for i in range(0, 192, step):
                at = 192 * a + i
                part[k, at // shard, at % shard : at % shard + step] = joint[i : i + step]
        for t in range(nt):
            ab_s[k, t] = part[k, t].astype(BF)
        stage[k] = [send(ab_s.at[k, peer[0]], ab_r.at[k, tm], peer) for peer in tms]

    def arrive(k):
        for copy in stage[k]:
            copy.wait()

    def scatter(k):
        arrive(k)
        value = part[k, tm]
        for d in range(1, nt):
            value = value + ab_r[k, (tm + d) % nt].astype(F32)
        flat_f[0:shard] = value
        for i in range(ns):
            rs_s[k, i] = flat_f[piece * i : piece * i + piece].astype(BF)
        stage[k] = [send(rs_s.at[k, peer[1]], rs_r.at[k, sp], peer) for peer in sps]

    def spread(k):
        arrive(k)
        value = rs_s[k, sp].astype(F32)
        for d in range(1, ns):
            value = value + rs_r[k, (sp + d) % ns].astype(F32)
        ag_b[k, tm, sp] = value.astype(BF)
        stage[k] = [send(ag_b.at[k, tm, sp], ag_b.at[k, tm, sp], peer) for peer in sps]

    def share(k):
        arrive(k)
        stage[k] = [send(ag_b.at[k, tm], ag_b.at[k, tm], peer) for peer in tms]

    def finish(k):
        arrive(k)
        for t in range(nt):
            for i in range(ns):
                flat_f[piece * i : piece * i + piece] = ag_b[k, t, i].astype(F32)
            wg_ref[k, t] = flat_f[0:shard].astype(BF)

    def hand_out(low, count):
        a, b = low * rows, (low + count) * rows
        for j in range(wide):
            cut = slice(768 + 256 * j, 1024 + 256 * j)
            flat = cot[2 : 2 + rows, half:, cut].reshape(low_rows, 256).astype(BF)
            out_r[tm, a:b, 256 * j : 256 * j + 256] = nn_dot(sel[a:b], flat).astype(BF)
        return [send(out_r.at[tm, a:b], out_r.at[tm, a:b], peer) for peer in xs + [sib]]

    def hand_on(low, count, copies):
        a, b = low * rows, (low + count) * rows
        later = copies[-1:]
        for i, copy in enumerate(copies[:-1]):
            copy.wait()
            source = ((xi + nx - 1 - i) % nx) * 2 + core
            later.append(send(out_r.at[source, a:b], out_r.at[source, a:b], sib))
        return later

    stage = {}
    quarter = rows // 4
    inner_one = [(2, rows - 2)]
    outer_one = [(0, 2), (rows, 2)]
    inner_two = [(quarter, rows - 2 * quarter)]
    outer_two = [(0, quarter), (rows - quarter, quarter)]

    def tile(k):
        return 0 if k == levels - 1 else half

    def put_grad(k):
        g = tile(k)

        def store(r, j, block):
            cut = slice(256 * j, 256 * j + 256)
            work[r, :, cut] = (block * slope[r, g : g + 8, cut]).astype(BF).astype(F32)

        return store

    def put_refs(r, j, block):
        cut = slice(256 * j, 256 * j + 256)
        refs[r, :, cut] = block * inside[:, cut]

    def combine(k, spans, base, width):
        for j in range(base, base + width):
            cut = slice(256 * j, 256 * j + 256)
            block = jnp.concatenate([refs[low : low + count, :, cut].reshape(count * 8, 256)
                                     for low, count in spans], axis=0).astype(BF)
            extra = nn_dot(comb[k], block)
            at = 0
            for low, count in spans:
                cot[2 + low : 2 + low + count, half:, cut] += extra[
                    at : at + count * half].reshape(count, half, 256)
                at += count * half

    def bounds(k, n):
        skip = 2 - -(-(2 * k + 1 - n) // 4)
        return 1 + skip, inner_q - 2 * skip

    def first(k, cells, landed):
        base, width = bounds(k, 0)
        fill(im, cot, tile(k), 0, landed, base, width)
        conv(im, 0, k, cells, base, width, put_grad(k))

    def second(k, cells, landed):
        base, width = bounds(k, 1)
        fill(imw, work, 0, 0, landed, base, width)
        conv(imw, 1, k, cells, base, width, put_refs)
        combine(k, cells, base, width)

    top_level = levels - 1
    for r in range(1, rows + 1):
        activate(r)
    first(top_level, inner_one, [(2, rows)])
    settle(edges)
    pre[1, :, mid] = pre_r[0].astype(F32) * has_up
    pre[rows + 2, :, mid] = pre_r[1].astype(F32) * has_down
    activate(0)
    activate(rows + 1)
    moving = []
    for k in range(top_level, -1, -1):
        land(k, flight)
        first(k, outer_one, [(0, 2), (rows + 2, 2)])
        if k == 0:
            keep_pair(0)
            correlate(0)
            scatter(1)
        second(k, outer_two, [(0, rows + 2)])
        if k > 0:
            flight = push(k - 1)
        if k == 1:
            scatter(3)
            scatter(2)
        second(k, inner_two, [])
        if k > 0:
            keep_pair(k)
            first(k - 1, inner_one, [(2, rows)])
        if k == 3:
            fill(imc.at[1, 0], act, 0, 1, [(0, rows + 2)], 3, wide)
            fill(imc.at[1, 1], act, half, 1, [(0, rows + 2)], 3, wide)
            moving.append((segs[0], hand_out(*segs[0])))
            gather(2)
            trim = slice(640, 896 + own)
            mix_s[0] = mix[2, :, trim].astype(BF)
            mix_s[1] = mix[rows + 1, :, trim].astype(BF)
            edges = exchange(mix_s, mix_r)
        if k == 2:
            moving.append((segs[1], hand_out(*segs[1])))
            moving[0] = (segs[0], hand_on(*moving[0][0], moving[0][1]))
            settle(edges)
            mix[1, :, trim] = mix_r[0].astype(F32) * has_up
            mix[rows + 2, :, trim] = mix_r[1].astype(F32) * has_down
            fill(imc.at[0, 0], mix, 0, 1, [(0, rows + 2)], 3, wide)
            fill(imc.at[0, 1], mix, half, 1, [(0, rows + 2)], 3, wide)
            correlate(3)
            correlate(2)
        if k == 1:
            moving[1] = (segs[1], hand_on(*moving[1][0], moving[1][1]))
            correlate(1)
            spread(3)
            spread(2)
    moving.append((segs[2], hand_out(*segs[2])))
    scatter(0)
    spread(1)
    share(3)
    share(2)
    moving[2] = (segs[2], hand_on(*moving[2][0], moving[2][1]))
    spread(0)
    share(1)
    loads[5].wait()
    finish(3)
    finish(2)
    share(0)
    for _, copies in moving:
        for copy in copies:
            copy.wait()
    for t in range(nt):
        for j in range(wide):
            cut = slice(own * t + 256 * j, own * t + 256 * j + 256)
            plain = whole[:, :, cut].astype(F32).reshape(fl * rows, 256)
            value = nn_dot(back[...], out_r[t, :, 256 * j : 256 * j + 256]) + top * plain
            grad_ref[:, cut] = value.astype(BF)
    finish(1)
    finish(0)


def widen_kernel(grad_ref, wg_ref, out_ref, one_ref, two_ref):
    out_ref[...] = grad_ref[...].astype(F32)
    one_ref[...] = wg_ref[:, 0:64].astype(F32)
    two_ref[...] = wg_ref[:, 64:128].astype(F32)


def on_device(cotangent, saved_mix, saved_pre, kernel_one, kernel_two, ref_pairs, frame_level):
    fl, rows, width = cotangent.shape
    nt = lax.axis_size("tm")
    nx = nt // 2
    ns = lax.axis_size("space")
    levels = kernel_one.shape[0]
    frames = fl * nt
    half = frames // 2
    own = width // nt
    lanes = own + 1536
    span = own + 1024
    quads = lanes // 256
    wide = own // 256
    chip = 2 * own + (512 if nx <= 2 else 1024)
    shard = 576 // nt
    tall = rows + 4
    few = rows // 2 * half
    vmem = pl.BlockSpec(memory_space=pltpu.VMEM)
    hbm = pl.BlockSpec(memory_space=pl.ANY)
    piece = -(-shard // ns)
    count = (3 * (nx - 1) + 3 * nx + 4 + 2 * levels + (levels - 1) * (2 * nx - 1)
             + 2 * levels * (nt - 1 + ns - 1))
    halo = [pltpu.VMEM((2, 2 * 2**k, own + 256 * (k + 1)), BF) for k in range(levels)]
    grad, wg = pl.pallas_call(
        functools.partial(group_kernel, nx, ns, levels),
        out_shape=(
            jax.ShapeDtypeStruct((fl * rows, width), BF),
            jax.ShapeDtypeStruct((levels, nt, shard, 128), BF),
        ),
        in_specs=[hbm] * 3 + [vmem] * 2 + [hbm] * 2,
        out_specs=(vmem, vmem),
        scratch_shapes=[
            pltpu.VMEM((3, nx, fl, rows, chip + 1024), BF),
            pltpu.VMEM((3, nx, fl, rows, span), BF),
            pltpu.VMEM((2, frames, span), BF),
            pltpu.VMEM((2, frames, span), BF),
            pltpu.VMEM((2, frames, own + 256), BF),
            pltpu.VMEM((2, frames, own + 256), BF),
            pltpu.VMEM((tall, frames, lanes), F32),
            pltpu.VMEM((tall, frames, lanes), F32),
            pltpu.VMEM((tall, frames, lanes), F32),
            pltpu.VMEM((tall, frames, lanes), F32),
            pltpu.VMEM((rows + 2, frames, lanes), F32),
            pltpu.VMEM((rows + 2, 8, lanes), F32),
            pltpu.VMEM((rows, 8, lanes), F32),
            pltpu.VMEM((tall, 8 * (quads - 2), 512), BF),
            pltpu.VMEM((rows + 2, 8 * (quads - 2), 512), BF),
            pltpu.VMEM((2, 2, rows + 2, 8 * wide, 512), BF),
            pltpu.VMEM(((rows - 2) * 8 * (quads - 2), 256), F32),
            pltpu.VMEM((nt, rows * half, own), BF),
            pltpu.VMEM((levels, 2, rows, 8 * wide, 256), BF),
            pltpu.VMEM((2, levels, 3, 512, 256), BF),
            pltpu.VMEM((320, 64), BF),
            pltpu.VMEM((rows * frames, rows * frames), BF),
            pltpu.VMEM((levels, few, few), BF),
            pltpu.VMEM((rows * half, rows * half), BF),
            pltpu.VMEM((fl * rows, rows * half), BF),
            pltpu.VMEM((levels, nt, shard, 128), F32),
            pltpu.VMEM((levels, nt, shard, 128), BF),
            pltpu.VMEM((levels, nt, shard, 128), BF),
            pltpu.VMEM((levels, ns, piece, 128), BF),
            pltpu.VMEM((levels, ns, piece, 128), BF),
            pltpu.VMEM((levels, nt, ns, piece, 128), BF),
            pltpu.VMEM((ns * piece, 128), F32),
            pltpu.VMEM((fl, rows, width), BF),
            pltpu.VMEM((levels, 3, 192, 64), BF),
            pltpu.VMEM((levels, 3, 192, 64), BF),
            pltpu.SemaphoreType.DMA((6,)),
            pltpu.SemaphoreType.DMA((count,)),
            pltpu.SemaphoreType.DMA((count,)),
        ] + halo + halo,
        compiler_params=pltpu.CompilerParams(
            collective_id=3, has_side_effects=True, vmem_limit_bytes=60 * 2**20
        ),
        name="group",
    )(cotangent, saved_pre, saved_mix, frame_level.reshape(1, frames), ref_pairs.T,
      kernel_one.reshape(levels, 3, 192, 64), kernel_two.reshape(levels, 3, 192, 64))
    grad, one, two = pl.pallas_call(
        widen_kernel,
        grid=(levels,),
        out_shape=(
            jax.ShapeDtypeStruct((fl * rows, width), F32),
            jax.ShapeDtypeStruct((levels * 576, 64), F32),
            jax.ShapeDtypeStruct((levels * 576, 64), F32),
        ),
        in_specs=[pl.BlockSpec((fl * rows, width // levels), lambda i: (0, i)),
                  pl.BlockSpec((576, 128), lambda i: (i, 0))],
        out_specs=(pl.BlockSpec((fl * rows, width // levels), lambda i: (0, i)),
                   pl.BlockSpec((576, 64), lambda i: (i, 0)),
                   pl.BlockSpec((576, 64), lambda i: (i, 0))),
        name="widen",
    )(grad, wg.reshape(levels * 576, 128))
    return (grad.reshape(cotangent.shape), one.reshape(kernel_one.shape),
            two.reshape(kernel_one.shape))


def solution(mesh):
    placed = (
        P("tm", "space", None),
        P("tm", "space", None),
        P("tm", "space", None),
        P(),
        P(),
        P(),
        P(),
    )
    return jax.shard_map(
        on_device,
        mesh=mesh,
        in_specs=placed,
        out_specs=(P("tm", "space", None), P(), P()),
        check_vma=False,
    )
```
